256 devices in a mesh: pool: 2 (over core), seq: 16 (over x, y), head: 8 (over z).
Axes of the slice: x: 4, y: 4, z: 8, core: 2. Of those that a mesh axis runs over, the one named last changes fastest.
Arguments:
- x_in: bfloat16 [1, 16384, 8, 2048], P(None, 'seq', 'head', 'pool'), may hold values from -6 to 6
- gate_in: bfloat16 [1, 16384, 8, 2048], P(None, 'seq', 'head', 'pool'), may hold values from -6 to 6
- dt_raw: bfloat16 [1, 16384, 8, 32], P(None, 'seq', 'head', 'pool'), may hold values from -4 to 4
- b_in: bfloat16 [1, 16384, 8, 256], P(None, 'seq', 'head'), may hold values from -0.375 to 0.375
- c_in: bfloat16 [1, 16384, 8, 256], P(None, 'seq', 'head'), may hold values from -6 to 6
- lengths: int32 [1], replicated, may hold values from 4096 to 16384
- decay_rate: float32 [8, 32], P('head', 'pool'), may hold values from 0.0001 to 0.05
- skip_gain: float32 [8, 32], P('head', 'pool'), may hold values from 0.5 to 2
- norm_gain: float32 [8, 2048], P('head', 'pool'), may hold values from 0.5 to 1.5
- dec_states: float32 [64, 8, 32, 64, 256], P('seq', 'head', 'pool'), may hold values from -18 to 18
- dec_x: bfloat16 [8, 64, 8, 2048], P(None, 'seq', 'head', 'pool'), may hold values from -6 to 6
- dec_gate: bfloat16 [8, 64, 8, 2048], P(None, 'seq', 'head', 'pool'), may hold values from -6 to 6
- dec_dt: bfloat16 [8, 64, 8, 32], P(None, 'seq', 'head', 'pool'), may hold values from -4 to 4
- dec_b: bfloat16 [8, 64, 8, 256], P(None, 'seq', 'head'), may hold values from -0.375 to 0.375
- dec_c: bfloat16 [8, 64, 8, 256], P(None, 'seq', 'head'), may hold values from -6 to 6
- slots: int32 [64], P('seq'), may hold values from -1 to 0, as said below
Outputs:
- prefill_out: bfloat16 [1, 16384, 8, 2048], P(None, 'seq', 'head', 'pool')
- decode_out: bfloat16 [8, 64, 8, 2048], P(None, 'seq', 'head', 'pool')
The draws below stay inside these ranges and needn't reach their ends.
Inputs may be any that keep to these rules, and one draw needn't show every extreme that they name: `lengths`: valid positions of each prompt; later positions are padding. `slots`: each aligned block of 4 decode sequences holds at least one that continues a prompt and at least one that keeps its own state.
All inputs are finite; a program needn't handle non-finite values.
Results may differ from the reference program's by a relative error of at most 0.001.
Values sent between devices are 32-bit elements; how exact they have to be, the bound alone decides.
No kernel may reach another device: no remote copies, remote signals or barrier semaphores. Data moves between devices by JAX's collectives and lax.ppermute only.
A program may use at most 128 MiB of HBM per device.

```python
import math
import jax
import jax.numpy as jnp
from jax import lax

HEADS = 256
HEAD_DIM = 64
STATE = 256
GROUPS = 8
PROMPTS = 1
SPAN = 256
DEC_DEV = 4
STEPS = 8
LENGTH = 16384
DECODES = 64


def draw_slots(key, part):
    first_key, second_key, third_key = jax.random.split(jax.random.fold_in(key, 11), 3)
    block_count = DECODES // DEC_DEV
    base = jax.random.randint(first_key, (DECODES,), -1, PROMPTS)
    offset = jax.random.randint(second_key, (block_count,), 0, DEC_DEV)
    chosen = jax.random.randint(third_key, (block_count,), 0, PROMPTS)
    rows = jnp.arange(DECODES, dtype=jnp.int32)
    block_of = rows // DEC_DEV
    inside = rows % DEC_DEV
    place = offset[block_of]
    result = jnp.where(inside == place, chosen[block_of], jnp.where(inside == (place + 1) % DEC_DEV, -1, base))
    return result.astype(jnp.int32)


def level_of(stream_key, extent, cuts, smallest, top_value):
    def one(position, blocks):
        steps = jax.random.uniform(jax.random.fold_in(jax.random.fold_in(stream_key, 6), position), (blocks,), jnp.float32, smallest / len(cuts), top_value / len(cuts))
        return jnp.repeat(jnp.exp(steps), extent[position] // blocks).reshape((-1,) + (1,) * (len(extent) - position - 1))

    level = one(*cuts[0])
    for cut in cuts[1:]:
        level = level * one(*cut)
    return level


def centred(key, dims, spread, limit, pieces=(), kind=jnp.bfloat16):
    values = spread * jax.random.normal(key, dims, jnp.float32)
    if pieces:
        values = values * level_of(key, dims, pieces, -0.22, 0.18)
    return jnp.clip(values, -limit, limit).astype(kind)


def setup_inputs(seed: int = 0) -> dict:
    arg_keys = jax.random.split(jax.random.key(seed), 17)
    return {
        "x_in": centred(arg_keys[0], (PROMPTS, LENGTH, GROUPS, HEADS // GROUPS * HEAD_DIM), 1.0, 6.0, ((1, 16), (2, 8), (3, 2))),
        "gate_in": centred(arg_keys[1], (PROMPTS, LENGTH, GROUPS, HEADS // GROUPS * HEAD_DIM), 1.0, 6.0, ((1, 16), (2, 8), (3, 2))),
        "dt_raw": centred(arg_keys[2], (PROMPTS, LENGTH, GROUPS, HEADS // GROUPS), 1.0, 4.0, ((1, 16), (2, 8), (3, 2))),
        "b_in": centred(arg_keys[3], (PROMPTS, LENGTH, GROUPS, STATE), STATE ** -0.5, 0.375, ((1, 16), (2, 8))),
        "c_in": centred(arg_keys[4], (PROMPTS, LENGTH, GROUPS, STATE), 1.0, 6.0, ((1, 16), (2, 8))),
        "lengths": jax.random.randint(arg_keys[5], (PROMPTS,), LENGTH // 4, LENGTH + 1).astype(jnp.int32),
        "decay_rate": jnp.clip(jnp.exp(math.log(0.05) - 6.214608 * jax.random.uniform(arg_keys[6], (GROUPS, HEADS // GROUPS), jnp.float32) ** level_of(arg_keys[6], (GROUPS, HEADS // GROUPS), ((0, 8), (1, 2)), -0.2, 0.2)), 0.0001, 0.05),
        "skip_gain": jnp.clip(0.5 + 1.5 * jax.random.uniform(arg_keys[7], (GROUPS, HEADS // GROUPS), jnp.float32) ** level_of(arg_keys[7], (GROUPS, HEADS // GROUPS), ((0, 8), (1, 2)), -0.2, 0.2), 0.5, 2.0),
        "norm_gain": jnp.clip(1.0 + 0.1 * jax.random.normal(arg_keys[8], (GROUPS, HEADS // GROUPS * HEAD_DIM), jnp.float32), 0.5, 1.5),
        "dec_states": centred(arg_keys[9], (DECODES, GROUPS, HEADS // GROUPS, HEAD_DIM, STATE), 3.0, 18.0, ((0, 16), (1, 8), (2, 2)), jnp.float32),
        "dec_x": centred(arg_keys[10], (STEPS, DECODES, GROUPS, HEADS // GROUPS * HEAD_DIM), 1.0, 6.0, ((1, 16), (2, 8), (3, 2))),
        "dec_gate": centred(arg_keys[11], (STEPS, DECODES, GROUPS, HEADS // GROUPS * HEAD_DIM), 1.0, 6.0, ((1, 16), (2, 8), (3, 2))),
        "dec_dt": centred(arg_keys[12], (STEPS, DECODES, GROUPS, HEADS // GROUPS), 1.0, 4.0, ((1, 16), (2, 8), (3, 2))),
        "dec_b": centred(arg_keys[13], (STEPS, DECODES, GROUPS, STATE), STATE ** -0.5, 0.375, ((1, 16), (2, 8))),
        "dec_c": centred(arg_keys[14], (STEPS, DECODES, GROUPS, STATE), 1.0, 6.0, ((1, 16), (2, 8))),
        "slots": draw_slots(jax.random.fold_in(arg_keys[16], 71), 0),
    }


highest = lax.Precision.HIGHEST
epsilon = 1e-05

def gated_norm(values, gate_part, gain_part):
    mixed = values * jax.nn.silu(gate_part.astype(jnp.float32))
    power = lax.optimization_barrier(jnp.mean(mixed * mixed, axis=-1, keepdims=True))
    return mixed * lax.rsqrt(power + epsilon) * gain_part

def reference(x_in, gate_in, dt_raw, b_in, c_in, lengths, decay_rate, skip_gain, norm_gain, dec_states, dec_x, dec_gate, dec_dt, dec_b, dec_c, slots):
    per_group = HEADS // GROUPS
    spans = LENGTH // SPAN
    live_mask = (jnp.arange(LENGTH, dtype=jnp.int32)[None, :] < lengths[:, None]).astype(jnp.float32)
    step_size = jax.nn.softplus(dt_raw.astype(jnp.float32)) * live_mask[:, :, None, None]
    log_decay = -step_size * decay_rate
    values = x_in.astype(jnp.float32).reshape(PROMPTS, LENGTH, GROUPS, per_group, HEAD_DIM)
    inflow = values * step_size[..., None]

    def blocks(array):
        return jnp.swapaxes(array.reshape((PROMPTS, spans, SPAN) + array.shape[2:]), 0, 1)
    positions = jnp.arange(SPAN)
    lower_mask = positions[:, None] >= positions[None, :]

    def span_step(running, inputs):
        flow, vals, b_part, c_part, logs, alive = inputs
        cumulative = jnp.moveaxis(jnp.cumsum(logs, axis=1), 1, -1)
        scores = jnp.einsum('bign,bjgn->bgij', c_part, b_part, precision=highest)
        gaps = cumulative[..., :, None] - cumulative[..., None, :]
        weights = jnp.exp(jnp.where(lower_mask, gaps, -jnp.inf)) * scores[:, :, None]
        inner = jnp.einsum('bghij,bjghp->bighp', weights, flow, precision=highest)
        outer = jnp.einsum('bign,bghpn->bghip', c_part, running, precision=highest) * jnp.exp(cumulative)[..., None]
        outer = jnp.transpose(outer, (0, 3, 1, 2, 4))
        output = (inner + outer + skip_gain[:, :, None] * vals) * alive[:, :, None, None, None]
        last = cumulative[..., -1:]
        carried = jnp.einsum('bjghp,bjgn,bghj->bghpn', flow, b_part, jnp.exp(last - cumulative), precision=highest)
        running = running * jnp.exp(last)[..., None] + carried
        return (running, output)
    initial = jnp.zeros((PROMPTS, GROUPS, per_group, HEAD_DIM, STATE), jnp.float32)
    final, outputs = lax.scan(span_step, initial, (blocks(inflow), blocks(values), blocks(b_in.astype(jnp.float32)), blocks(c_in.astype(jnp.float32)), blocks(log_decay), blocks(live_mask)))
    outputs = jnp.swapaxes(outputs, 0, 1).reshape(PROMPTS, LENGTH, GROUPS, per_group * HEAD_DIM)
    prefill_out = gated_norm(outputs, gate_in, norm_gain).astype(jnp.bfloat16)
    inserted = final[jnp.maximum(slots, 0).astype(jnp.int32)]
    start = jnp.where((slots >= 0)[:, None, None, None, None], inserted, dec_states)

    def decode_step(states, inputs):
        x_step, gate_step, dt_step, b_step, c_step = inputs
        step_dt = jax.nn.softplus(dt_step.astype(jnp.float32))
        vals = x_step.astype(jnp.float32).reshape(DECODES, GROUPS, per_group, HEAD_DIM)
        keep = jnp.exp(-step_dt * decay_rate)
        flow = vals * step_dt[..., None]
        states = states * keep[..., None, None] + flow[..., None] * b_step.astype(jnp.float32)[:, :, None, None, :]
        result = jnp.einsum('dgn,dghpn->dghp', c_step.astype(jnp.float32), states, precision=highest) + skip_gain[..., None] * vals
        normed = gated_norm(result.reshape(DECODES, GROUPS, per_group * HEAD_DIM), gate_step, norm_gain)
        return (states, normed.astype(jnp.bfloat16))
    end_states, decode_out = lax.scan(decode_step, start, (dec_x, dec_gate, dec_dt, dec_b, dec_c))
    return (prefill_out, decode_out)
```

```python
import jax
import jax.numpy as jnp
from jax import lax
from jax.experimental import pallas as pl
from jax.experimental.pallas import tpu as pltpu
from jax.sharding import Mesh
from jax.sharding import PartitionSpec as P

SEQ = ("seq_0", "seq_1")
HEAD_DIM = 64
SPAN = 256
TILE = 128
EPS = 1e-05
F32 = jnp.float32
BF16 = jnp.bfloat16


def iota(shape, dim):
    return lax.broadcasted_iota(jnp.int32, shape, dim)


def dot(a, b, ca, cb):
    return lax.dot_general(a, b, (((ca,), (cb,)), ((), ())), preferred_element_type=F32)


def exact_dot(a, b):
    return jnp.dot(a, b, precision=lax.Precision.HIGHEST, preferred_element_type=F32)


def split2(v):
    hi = v.astype(BF16)
    return hi, (v - hi.astype(F32)).astype(BF16)


def split3(v):
    hi = v.astype(BF16)
    rest = v - hi.astype(F32)
    mid = rest.astype(BF16)
    low = (rest - mid.astype(F32)).astype(BF16)
    return jnp.concatenate([hi, mid, low], axis=0)


def spread(heads, width):
    one = iota((heads, width), 0) == iota((heads, width), 1) // HEAD_DIM
    return jnp.where(one, 1.0, 0.0)


def spread3(heads, width):
    one = spread(heads, width).astype(BF16)
    return jnp.concatenate([one, one, one], axis=0)


def per_channel(v, table):
    return dot(split3(v), table, 0, 0)


def as_column(row):
    n = row.shape[1]
    return jnp.sum(jnp.where(iota((n, n), 0) == iota((n, n), 1), row, 0.0), axis=1, keepdims=True)


def as_row(column, width):
    n = column.shape[0]
    same = iota((n, width), 0) == iota((n, width), 1)
    return jnp.sum(jnp.where(same, column, 0.0), axis=0, keepdims=True)


def silu(v):
    return v * jax.nn.sigmoid(v)


def head_terms(dt_ref, rate, first, limit):
    heads, span = dt_ref.shape
    live = first + iota((heads, span), 1) < limit
    step = jnp.where(live, jax.nn.softplus(dt_ref[...].astype(F32)), 0.0)
    upper = jnp.where(iota((span, span), 0) <= iota((span, span), 1), 1.0, 0.0).astype(BF16)
    sums = dot(split3(-step * rate), upper, 1, 0)
    return step, sums[:heads] + sums[heads : 2 * heads] + sums[2 * heads :]


def state_kernel(limit_ref, rate_ref, dt_ref, x_ref, b_ref, dec_c_ref, out_ref, state, total):
    t = pl.program_id(0)
    heads, span = dt_ref.shape
    width = x_ref.shape[1]

    @pl.when(t == 0)
    def _():
        state[...] = jnp.zeros_like(state)
        total[...] = jnp.zeros_like(total)

    table = spread3(heads, width)
    step, cum = head_terms(dt_ref, as_column(rate_ref[...]), t * span, limit_ref[0])
    last = cum[:, span - 1 :]
    flow = x_ref[...].astype(F32) * per_channel(step * jnp.exp(last - cum), table)
    high, low = split2(flow)
    b = b_ref[...]
    new_total = total[...] + last
    total[...] = new_total
    lane = iota((heads, TILE), 1)
    rows = per_channel(jnp.where(lane < 8, jnp.exp(last), jnp.exp(new_total)), table)
    new = state[...] * rows[0:1] + (dot(b, high, 0, 0) + dot(b, low, 0, 0))
    state[...] = new

    @pl.when(t == pl.num_programs(0) - 1)
    def _():
        wide = width // TILE
        steps, rows_dec, _ = dec_c_ref.shape
        for half in range(new.shape[0] // TILE):
            for col in range(wide):
                j = half * wide + col
                at = (pl.ds(half * TILE, TILE), pl.ds(col * TILE, TILE))
                out_ref[j, :TILE, :] = state[at]
                out_ref[j, TILE : TILE + 8, :] = rows[8:16, col * TILE : (col + 1) * TILE]
                for s in range(steps):
                    base = TILE + 8 + s * rows_dec
                    out_ref[j, base : base + rows_dec, :] = dec_c_ref[
                        s, :, half * TILE : (half + 1) * TILE
                    ].astype(F32)


def prefix_kernel(in_ref, out_ref):
    count = in_ref.shape[0]
    dec = in_ref.shape[1] - TILE - 8
    state = jnp.zeros((TILE, TILE), F32)
    for k in range(count):
        out_ref[k, :TILE, :] = state
        state = state * in_ref[k, TILE : TILE + 1, :] + in_ref[k, :TILE, :]
    high, low = split2(state)
    c = in_ref[:, TILE + 8 :, :].reshape(count * dec, TILE).astype(BF16)
    y = dot(c, high, 1, 0) + dot(c, low, 1, 0)
    out_ref[:, TILE:, :] = y.reshape(count, dec, TILE)


def local_kernel(
    limit_ref, rate_ref, skip_ref, dt_ref, x_ref, gate_ref, b_ref, c_ref,
    part_ref, coef_ref, state, total, skip,
):
    t = pl.program_id(0)
    heads, span = dt_ref.shape
    width = x_ref.shape[1]

    @pl.when(t == 0)
    def _():
        state[...] = jnp.zeros_like(state)
        total[...] = jnp.zeros_like(total)
        skip[...] = exact_dot(
            jnp.broadcast_to(skip_ref[...], (8, heads)), spread(heads, width)
        )

    table = spread3(heads, width)
    step, cum = head_terms(dt_ref, as_column(rate_ref[...]), t * span, limit_ref[0])
    last = cum[:, span - 1 :]
    b, c = b_ref[...], c_ref[...]
    x = x_ref[...].astype(F32)
    high, low = split2(x * per_channel(step * jnp.exp(-cum), table))
    lower = iota((span, span), 0) >= iota((span, span), 1)
    score_high, score_low = split2(jnp.where(lower, dot(c, b, 1, 1), 0.0))
    acc = dot(score_high, high, 1, 0) + dot(score_high, low, 1, 0) + dot(score_low, high, 1, 0)
    now = state[...]
    now_high, now_low = split2(now)
    acc = acc + dot(c, now_high, 1, 0) + dot(c, now_low, 1, 0)
    decay = per_channel(jnp.exp(cum), table)
    before = total[...]
    total[...] = before + last
    lane = iota((heads, TILE), 1)
    rows = per_channel(jnp.where(lane < 8, jnp.exp(last), jnp.exp(before)), table)
    live = t * span + iota((span, width), 0) < limit_ref[0]
    gate = jnp.where(live, silu(gate_ref[...].astype(F32)), 0.0)
    part_ref[...] = (acc * decay + skip[0:1] * x) * gate
    coef_ref[...] = decay * rows[8:9] * gate
    state[...] = (now + (dot(b, high, 0, 0) + dot(b, low, 0, 0))) * rows[0:1]


def decode_kernel(
    slots_ref, rate_ref, skip_ref, dt_ref, x_ref, gate_ref, b_ref, c_ref, state_ref,
    part_ref, coef_ref, x_all, gate_all, b_all, c_all, keep_log, size_all,
):
    d = pl.program_id(0)
    steps, seqs, width = x_ref.shape
    heads = dt_ref.shape[2]
    rows = steps * seqs

    @pl.when(d == 0)
    def _():
        total = jnp.zeros((seqs, heads), F32)
        for s in range(steps):
            at = pl.ds(s * seqs, seqs)
            size = jax.nn.softplus(dt_ref[s].astype(F32))
            total = total - size * rate_ref[...]
            keep_log[at, :] = total
            size_all[at, :] = size
            x_all[at, :] = x_ref[s].astype(F32)
            gate_all[at, :] = gate_ref[s].astype(F32)
            b_all[at, :] = b_ref[s].astype(F32)
            c_all[at, :] = c_ref[s].astype(F32)
        table = spread(heads, width)
        keep = exact_dot(jnp.exp(keep_log[...]), table)
        flow = exact_dot(size_all[...] * jnp.exp(-keep_log[...]), table) * x_all[...]
        scores = dot(c_all[...].astype(BF16), b_all[...].astype(BF16), 1, 1)
        row, col = iota((rows, rows), 0), iota((rows, rows), 1)
        same = (row % seqs == col % seqs) & (col <= row)
        inner = exact_dot(jnp.where(same, scores, 0.0), flow)
        skip = exact_dot(jnp.broadcast_to(skip_ref[...], (8, heads)), table)[0:1]
        gate = silu(gate_all[...])
        part_ref[...] = (keep * inner + skip * x_all[...]) * gate
        coef_ref[...] = keep * gate

    c = c_all[...].astype(BF16)
    high, low = split2(state_ref[0])
    own = dot(c, high, 1, 1) + dot(c, low, 1, 1)
    mine = iota((rows, 1), 0) % seqs == d
    take = mine & (slots_ref[d] < 0)
    part_ref[...] += jnp.where(take, own * coef_ref[...], 0.0)
    coef_ref[...] = jnp.where(take, 0.0, coef_ref[...])


def mix_kernel(
    in_ref, c_ref, part_ref, coef_ref, dec_part_ref, dec_coef_ref,
    mixed_ref, dec_mixed_ref, power_ref, high, low,
):
    t = pl.program_id(0)
    span = c_ref.shape[0]
    wide = part_ref.shape[1] // TILE

    @pl.when(t == 0)
    def _():
        power = jnp.zeros((dec_part_ref.shape[0], TILE), F32)
        for col in range(wide):
            cols = pl.ds(col * TILE, TILE)
            for half in range(in_ref.shape[0] // wide):
                at = (pl.ds(half * TILE, TILE), cols)
                high[at], low[at] = split2(in_ref[half * wide + col, :TILE, :])
            final = in_ref[col, TILE:, :] + in_ref[wide + col, TILE:, :]
            mixed = dec_part_ref[:, cols] + dec_coef_ref[:, cols] * final
            dec_mixed_ref[:, cols] = mixed
            power = power + mixed * mixed
        power_ref[...] = jnp.zeros_like(power_ref)
        power_ref[4:5, :] = as_row(jnp.sum(power, axis=1, keepdims=True), span)

    c = c_ref[...]
    mixed = part_ref[...] + coef_ref[...] * (dot(c, high[...], 1, 0) + dot(c, low[...], 1, 0))
    mixed_ref[...] = mixed
    power_ref[pl.ds(t, 1), :] = as_row(jnp.sum(mixed * mixed, axis=1, keepdims=True), span)


def norm_kernel(power_ref, other_ref, gain_ref, mixed_ref, dec_mixed_ref, out_ref, dec_ref, dec):
    t = pl.program_id(0)
    full = 2 * mixed_ref.shape[1]

    def scale(row):
        power = power_ref[pl.ds(row, 1), :] + other_ref[pl.ds(row, 1), :]
        return as_column(lax.rsqrt(power / full + EPS))

    out_ref[...] = (mixed_ref[...] * scale(t) * gain_ref[...]).astype(BF16)

    @pl.when(t == 0)
    def _():
        steps, seqs, _ = dec_ref.shape
        rows = steps * seqs
        dec[...] = dec_mixed_ref[...] * scale(4)[:rows] * gain_ref[...]
        for s in range(steps):
            dec_ref[s] = dec[s * seqs : (s + 1) * seqs, :].astype(BF16)


def params(mib):
    return pltpu.CompilerParams(
        dimension_semantics=("arbitrary",), vmem_limit_bytes=mib * 2**20
    )


def whole(shape):
    return pl.BlockSpec(shape, lambda t: (0,) * len(shape))


def by_rows(shape):
    return pl.BlockSpec(shape, lambda t: (t,) + (0,) * (len(shape) - 1))


def shards(
    x_in, gate_in, dt_raw, b_in, c_in, lengths, decay_rate, skip_gain, norm_gain,
    dec_states, dec_x, dec_gate, dec_dt, dec_b, dec_c, slots,
):
    _, length, _, width = x_in.shape
    heads, state = dt_raw.shape[3], b_in.shape[3]
    steps, seqs = dec_x.shape[:2]
    rows = steps * seqs
    count = lax.axis_size(SEQ)
    spans = length // SPAN
    limit = lengths - lax.axis_index(SEQ) * length
    x, gate = x_in.reshape(length, width), gate_in.reshape(length, width)
    dt = dt_raw.reshape(length, heads).T
    b, c = b_in.reshape(length, state), c_in.reshape(length, state)
    dec_x, dec_gate = dec_x.reshape(steps, seqs, width), dec_gate.reshape(steps, seqs, width)
    dec_b, dec_c = dec_b.reshape(steps, seqs, state), dec_c.reshape(steps, seqs, state)
    dec_dt = dec_dt.reshape(steps, seqs, heads)
    smem = pl.BlockSpec(memory_space=pltpu.SMEM)
    dt_spec = pl.BlockSpec((heads, SPAN), lambda t: (0, t))
    head_spec = whole((1, heads))
    wide_spec, state_spec = by_rows((SPAN, width)), by_rows((SPAN, state))
    sent_rows = TILE + 8 + rows
    back_rows = TILE + rows

    sent = pl.pallas_call(
        state_kernel,
        name="device_state",
        out_shape=jax.ShapeDtypeStruct((count, sent_rows, TILE), F32),
        grid=(spans,),
        in_specs=[smem, head_spec, dt_spec, wide_spec, state_spec, whole((steps, seqs, state))],
        out_specs=whole((count, sent_rows, TILE)),
        scratch_shapes=[pltpu.VMEM((state, width), F32), pltpu.VMEM((heads, TILE), F32)],
        compiler_params=params(24),
        cost_estimate=pl.CostEstimate(
            flops=8 * length * state * width, bytes_accessed=6 * 2**20, transcendentals=0
        ),
    )(limit, decay_rate, dt, x, b, dec_c)
    owned = lax.all_to_all(sent, SEQ, 0, 0)

    part, coef = pl.pallas_call(
        local_kernel,
        name="device_outputs",
        out_shape=[jax.ShapeDtypeStruct((length, width), F32)] * 2,
        grid=(spans,),
        in_specs=[
            smem, head_spec, head_spec, dt_spec, wide_spec, wide_spec, state_spec, state_spec,
        ],
        out_specs=[wide_spec, wide_spec],
        scratch_shapes=[
            pltpu.VMEM((state, width), F32),
            pltpu.VMEM((heads, TILE), F32),
            pltpu.VMEM((8, width), F32),
        ],
        compiler_params=params(32),
        cost_estimate=pl.CostEstimate(
            flops=20 * length * state * width, bytes_accessed=14 * 2**20, transcendentals=0
        ),
    )(limit, decay_rate, skip_gain, dt, x, gate, b, c)

    dec_part, dec_coef = pl.pallas_call(
        decode_kernel,
        name="decode_own",
        out_shape=[jax.ShapeDtypeStruct((rows, width), F32)] * 2,
        grid=(seqs,),
        in_specs=[
            smem, head_spec, head_spec, whole((steps, seqs, heads)),
            whole((steps, seqs, width)), whole((steps, seqs, width)),
            whole((steps, seqs, state)), whole((steps, seqs, state)),
            by_rows((1, width, state)),
        ],
        out_specs=[whole((rows, width))] * 2,
        scratch_shapes=[
            pltpu.VMEM((rows, width), F32), pltpu.VMEM((rows, width), F32),
            pltpu.VMEM((rows, state), F32), pltpu.VMEM((rows, state), F32),
            pltpu.VMEM((rows, heads), F32), pltpu.VMEM((rows, heads), F32),
        ],
        compiler_params=params(16),
        cost_estimate=pl.CostEstimate(
            flops=4 * seqs * 256 * state * width, bytes_accessed=5 * 2**20, transcendentals=0
        ),
    )(
        slots, decay_rate, skip_gain, dec_dt, dec_x, dec_gate, dec_b, dec_c,
        dec_states.reshape(seqs, width, state),
    )

    back = pl.pallas_call(
        prefix_kernel,
        name="prefix",
        out_shape=jax.ShapeDtypeStruct((count, back_rows, TILE), F32),
        compiler_params=pltpu.CompilerParams(vmem_limit_bytes=16 * 2**20),
        cost_estimate=pl.CostEstimate(
            flops=2 * count * rows * TILE * TILE, bytes_accessed=3 * 2**20, transcendentals=0
        ),
    )(owned)
    entry = lax.all_to_all(back, SEQ, 0, 0)

    mixed, dec_mixed, power = pl.pallas_call(
        mix_kernel,
        name="mix",
        out_shape=[
            jax.ShapeDtypeStruct((length, width), F32),
            jax.ShapeDtypeStruct((rows, width), F32),
            jax.ShapeDtypeStruct((8, SPAN), F32),
        ],
        grid=(spans,),
        in_specs=[
            whole((count, back_rows, TILE)), state_spec, wide_spec, wide_spec,
            whole((rows, width)), whole((rows, width)),
        ],
        out_specs=[wide_spec, whole((rows, width)), whole((8, SPAN))],
        scratch_shapes=[pltpu.VMEM((state, width), BF16), pltpu.VMEM((state, width), BF16)],
        compiler_params=params(24),
        cost_estimate=pl.CostEstimate(
            flops=4 * length * state * width, bytes_accessed=14 * 2**20, transcendentals=0
        ),
    )(entry, c, part, coef, dec_part, dec_coef)
    other = lax.ppermute(power, "pool", [(0, 1), (1, 0)])

    prefill_out, decode_out = pl.pallas_call(
        norm_kernel,
        name="norm",
        out_shape=[
            jax.ShapeDtypeStruct((length, width), BF16),
            jax.ShapeDtypeStruct((steps, seqs, width), BF16),
        ],
        grid=(spans,),
        in_specs=[
            whole((8, SPAN)), whole((8, SPAN)), whole((1, width)), wide_spec, whole((rows, width)),
        ],
        out_specs=[wide_spec, whole((steps, seqs, width))],
        scratch_shapes=[pltpu.VMEM((rows, width), F32)],
        compiler_params=params(16),
        cost_estimate=pl.CostEstimate(
            flops=4 * length * width, bytes_accessed=6 * 2**20, transcendentals=0
        ),
    )(power, other, norm_gain, mixed, dec_mixed)
    return (
        prefill_out.reshape(x_in.shape),
        decode_out.reshape(steps, seqs, 1, width),
    )


def solution(mesh):
    split = Mesh(
        mesh.devices.reshape(mesh.shape["pool"], 4, 4, mesh.shape["head"]),
        ("pool", "seq_0", "seq_1", "head"),
    )
    wide = P(None, SEQ, "head", "pool")
    shared = P(None, SEQ, "head", None)
    per_head = P("head", "pool")
    return jax.shard_map(
        shards,
        mesh=split,
        in_specs=(
            wide, wide, wide, shared, shared, P(), per_head, per_head, per_head,
            P(SEQ, "head", "pool", None, None), wide, wide, wide, shared, shared, P(SEQ),
        ),
        out_specs=(wide, wide),
        check_vma=False,
    )
```

```python
import jax
import jax.numpy as jnp
from jax import lax
from jax.experimental import pallas as pl
from jax.experimental.pallas import tpu as pltpu
from jax.sharding import Mesh
from jax.sharding import PartitionSpec as P

SEQ = ("seq_0", "seq_1")
HEAD_DIM = 64
SPAN = 256
TILE = 128
EPS = 1e-05
F32 = jnp.float32
BF16 = jnp.bfloat16


def iota(shape, dim):
    return lax.broadcasted_iota(jnp.int32, shape, dim)


def dot(a, b, ca, cb):
    return lax.dot_general(a, b, (((ca,), (cb,)), ((), ())), preferred_element_type=F32)


def exact_dot(a, b):
    return jnp.dot(a, b, precision=lax.Precision.HIGHEST, preferred_element_type=F32)


def split2(v):
    hi = v.astype(BF16)
    return hi, (v - hi.astype(F32)).astype(BF16)


def split3(v):
    hi = v.astype(BF16)
    rest = v - hi.astype(F32)
    mid = rest.astype(BF16)
    low = (rest - mid.astype(F32)).astype(BF16)
    return jnp.concatenate([hi, mid, low], axis=0)


def spread(heads, width):
    one = iota((heads, width), 0) == iota((heads, width), 1) // HEAD_DIM
    return jnp.where(one, 1.0, 0.0)


def spread3(heads, width):
    one = spread(heads, width).astype(BF16)
    return jnp.concatenate([one, one, one], axis=0)


def per_channel(v, table):
    return dot(split3(v), table, 0, 0)


def as_column(row):
    n = row.shape[1]
    return jnp.sum(jnp.where(iota((n, n), 0) == iota((n, n), 1), row, 0.0), axis=1, keepdims=True)


def as_row(column, width):
    n = column.shape[0]
    same = iota((n, width), 0) == iota((n, width), 1)
    return jnp.sum(jnp.where(same, column, 0.0), axis=0, keepdims=True)


def silu(v):
    return v * jax.nn.sigmoid(v)


def head_terms(dt_ref, rate, first, limit):
    heads, span = dt_ref.shape
    live = first + iota((heads, span), 1) < limit
    step = jnp.where(live, jax.nn.softplus(dt_ref[...].astype(F32)), 0.0)
    upper = jnp.where(iota((span, span), 0) <= iota((span, span), 1), 1.0, 0.0).astype(BF16)
    sums = dot(split3(-step * rate), upper, 1, 0)
    return step, sums[:heads] + sums[heads : 2 * heads] + sums[2 * heads :]


def state_kernel(lengths_ref, rate_ref, dt_ref, x_ref, b_ref, dec_c_ref, out_ref, state, total):
    t = pl.program_id(0)
    heads, span = dt_ref.shape
    width = x_ref.shape[1]

    @pl.when(t == 0)
    def _():
        state[...] = jnp.zeros_like(state)
        total[...] = jnp.zeros_like(total)

    table = spread3(heads, width)
    limit = lengths_ref[0] - lax.axis_index(SEQ) * (pl.num_programs(0) * span)
    step, cum = head_terms(dt_ref, as_column(rate_ref[...]), t * span, limit)
    last = cum[:, span - 1 :]
    flow = x_ref[...].astype(F32) * per_channel(step * jnp.exp(last - cum), table)
    high, low = split2(flow)
    b = b_ref[...]
    new_total = total[...] + last
    total[...] = new_total
    lane = iota((heads, TILE), 1)
    rows = per_channel(jnp.where(lane < 8, jnp.exp(last), jnp.exp(new_total)), table)
    new = state[...] * rows[0:1] + (dot(b, high, 0, 0) + dot(b, low, 0, 0))
    state[...] = new

    @pl.when(t == pl.num_programs(0) - 1)
    def _():
        wide = width // TILE
        steps, rows_dec, _ = dec_c_ref.shape
        for half in range(new.shape[0] // TILE):
            for col in range(wide):
                j = half * wide + col
                at = (pl.ds(half * TILE, TILE), pl.ds(col * TILE, TILE))
                out_ref[j, :TILE, :] = state[at]
                out_ref[j, TILE : TILE + 8, :] = rows[8:16, col * TILE : (col + 1) * TILE]
                for s in range(steps):
                    base = TILE + 8 + s * rows_dec
                    out_ref[j, base : base + rows_dec, :] = dec_c_ref[
                        s, :, half * TILE : (half + 1) * TILE
                    ].astype(F32)


def prefix_kernel(in_ref, out_ref):
    count = in_ref.shape[0]
    dec = in_ref.shape[1] - TILE - 8
    state = jnp.zeros((TILE, TILE), F32)
    for k in range(count):
        out_ref[k, :TILE, :] = state
        state = state * in_ref[k, TILE : TILE + 1, :] + in_ref[k, :TILE, :]
    high, low = split2(state)
    c = in_ref[:, TILE + 8 :, :].reshape(count * dec, TILE).astype(BF16)
    y = dot(c, high, 1, 0) + dot(c, low, 1, 0)
    out_ref[:, TILE:, :] = y.reshape(count, dec, TILE)


def local_kernel(
    lengths_ref, rate_ref, skip_ref, dt_ref, x_ref, gate_ref, b_ref, c_ref,
    part_ref, state, total, skip,
):
    t = pl.program_id(0)
    heads, span = dt_ref.shape
    width = x_ref.shape[1]

    @pl.when(t == 0)
    def _():
        state[...] = jnp.zeros_like(state)
        total[...] = jnp.zeros_like(total)
        skip[...] = exact_dot(
            jnp.broadcast_to(skip_ref[...], (8, heads)), spread(heads, width)
        )

    table = spread3(heads, width)
    limit = lengths_ref[0] - lax.axis_index(SEQ) * (pl.num_programs(0) * span)
    step, cum = head_terms(dt_ref, as_column(rate_ref[...]), t * span, limit)
    last = cum[:, span - 1 :]
    b, c = b_ref[...], c_ref[...]
    x = x_ref[...].astype(F32)
    high, low = split2(x * per_channel(step * jnp.exp(-cum), table))
    lower = iota((span, span), 0) >= iota((span, span), 1)
    score_high, score_low = split2(jnp.where(lower, dot(c, b, 1, 1), 0.0))
    acc = dot(score_high, high, 1, 0) + dot(score_high, low, 1, 0) + dot(score_low, high, 1, 0)
    now = state[...]
    now_high, now_low = split2(now)
    acc = acc + dot(c, now_high, 1, 0) + dot(c, now_low, 1, 0)
    decay = per_channel(jnp.exp(cum), table)
    before = total[...]
    total[...] = before + last
    lane = iota((heads, TILE), 1)
    rows = per_channel(jnp.where(lane < 8, jnp.exp(last), jnp.exp(before)), table)
    live = t * span + iota((span, width), 0) < limit
    gate = jnp.where(live, silu(gate_ref[...].astype(F32)), 0.0)
    part_ref[0] = (acc * decay + skip[0:1] * x) * gate
    part_ref[1] = decay * rows[8:9] * gate
    state[...] = (now + (dot(b, high, 0, 0) + dot(b, low, 0, 0))) * rows[0:1]


def decode_kernel(
    slots_ref, rate_ref, skip_ref, dt_ref, x_ref, gate_ref, b_ref, c_ref, state_ref,
    part_ref, coef_ref, x_all, gate_all, b_all, c_all, keep_log, size_all,
):
    d = pl.program_id(0)
    steps, seqs, width = x_ref.shape
    heads = dt_ref.shape[2]
    rows = steps * seqs

    @pl.when(d == 0)
    def _():
        total = jnp.zeros((seqs, heads), F32)
        for s in range(steps):
            at = pl.ds(s * seqs, seqs)
            size = jax.nn.softplus(dt_ref[s].astype(F32))
            total = total - size * rate_ref[...]
            keep_log[at, :] = total
            size_all[at, :] = size
            x_all[at, :] = x_ref[s].astype(F32)
            gate_all[at, :] = gate_ref[s].astype(F32)
            b_all[at, :] = b_ref[s].astype(F32)
            c_all[at, :] = c_ref[s].astype(F32)
        table = spread(heads, width)
        keep = exact_dot(jnp.exp(keep_log[...]), table)
        flow = exact_dot(size_all[...] * jnp.exp(-keep_log[...]), table) * x_all[...]
        scores = dot(c_all[...].astype(BF16), b_all[...].astype(BF16), 1, 1)
        row, col = iota((rows, rows), 0), iota((rows, rows), 1)
        same = (row % seqs == col % seqs) & (col <= row)
        inner = exact_dot(jnp.where(same, scores, 0.0), flow)
        skip = exact_dot(jnp.broadcast_to(skip_ref[...], (8, heads)), table)[0:1]
        gate = silu(gate_all[...])
        part_ref[...] = (keep * inner + skip * x_all[...]) * gate
        coef_ref[...] = keep * gate

    c = c_all[...].astype(BF16)
    high, low = split2(state_ref[0])
    own = dot(c, high, 1, 1) + dot(c, low, 1, 1)
    mine = iota((rows, 1), 0) % seqs == d
    take = mine & (slots_ref[d] < 0)
    part_ref[...] += jnp.where(take, own * coef_ref[...], 0.0)
    coef_ref[...] = jnp.where(take, 0.0, coef_ref[...])


def mix_kernel(
    in_ref, c_ref, part_ref, dec_part_ref, dec_coef_ref,
    mixed_ref, dec_mixed_ref, power_ref, high, low,
):
    t = pl.program_id(0)
    span = c_ref.shape[0]
    wide = part_ref.shape[2] // TILE

    @pl.when(t == 0)
    def _():
        power = jnp.zeros((dec_part_ref.shape[0], TILE), F32)
        for col in range(wide):
            cols = pl.ds(col * TILE, TILE)
            for half in range(in_ref.shape[0] // wide):
                at = (pl.ds(half * TILE, TILE), cols)
                high[at], low[at] = split2(in_ref[half * wide + col, :TILE, :])
            final = in_ref[col, TILE:, :] + in_ref[wide + col, TILE:, :]
            mixed = dec_part_ref[:, cols] + dec_coef_ref[:, cols] * final
            dec_mixed_ref[:, cols] = mixed
            power = power + mixed * mixed
        power_ref[...] = jnp.zeros_like(power_ref)
        power_ref[4:5, :] = as_row(jnp.sum(power, axis=1, keepdims=True), span)

    c = c_ref[...]
    mixed = part_ref[0] + part_ref[1] * (dot(c, high[...], 1, 0) + dot(c, low[...], 1, 0))
    mixed_ref[...] = mixed
    power_ref[pl.ds(t, 1), :] = as_row(jnp.sum(mixed * mixed, axis=1, keepdims=True), span)


def norm_kernel(power_ref, other_ref, gain_ref, mixed_ref, dec_mixed_ref, out_ref, dec_ref, dec):
    t = pl.program_id(0)
    full = 2 * mixed_ref.shape[1]

    def scale(row):
        power = power_ref[pl.ds(row, 1), :] + other_ref[pl.ds(row, 1), :]
        return as_column(lax.rsqrt(power / full + EPS))

    out_ref[...] = (mixed_ref[...] * scale(t) * gain_ref[...]).astype(BF16)

    @pl.when(t == 0)
    def _():
        steps, seqs, _ = dec_ref.shape
        rows = steps * seqs
        dec[...] = dec_mixed_ref[...] * scale(4)[:rows] * gain_ref[...]
        for s in range(steps):
            dec_ref[s] = dec[s * seqs : (s + 1) * seqs, :].astype(BF16)


def params(mib):
    return pltpu.CompilerParams(
        dimension_semantics=("arbitrary",), vmem_limit_bytes=mib * 2**20
    )


def whole(shape):
    return pl.BlockSpec(shape, lambda t: (0,) * len(shape))


def by_rows(shape):
    return pl.BlockSpec(shape, lambda t: (t,) + (0,) * (len(shape) - 1))


def in_hbm(v):
    return pltpu.with_memory_space_constraint(v, pltpu.HBM)


def in_vmem(v):
    return pltpu.with_memory_space_constraint(v, pltpu.VMEM)


def shards(
    x_in, gate_in, dt_raw, b_in, c_in, lengths, decay_rate, skip_gain, norm_gain,
    dec_states, dec_x, dec_gate, dec_dt, dec_b, dec_c, slots,
):
    _, length, _, width = x_in.shape
    heads, state = dt_raw.shape[3], b_in.shape[3]
    steps, seqs = dec_x.shape[:2]
    rows = steps * seqs
    count = lax.axis_size(SEQ)
    spans = length // SPAN
    x, gate = x_in.reshape(length, width), gate_in.reshape(length, width)
    dt = dt_raw.reshape(length, heads).T
    b, c = b_in.reshape(length, state), c_in.reshape(length, state)
    dec_x, dec_gate = dec_x.reshape(steps, seqs, width), dec_gate.reshape(steps, seqs, width)
    dec_b, dec_c = dec_b.reshape(steps, seqs, state), dec_c.reshape(steps, seqs, state)
    dec_dt = dec_dt.reshape(steps, seqs, heads)
    smem = pl.BlockSpec(memory_space=pltpu.SMEM)
    dt_spec = pl.BlockSpec((heads, SPAN), lambda t: (0, t))
    head_spec = whole((1, heads))
    pair_spec = pl.BlockSpec((2, SPAN, width), lambda t: (0, t, 0))
    wide_spec, state_spec = by_rows((SPAN, width)), by_rows((SPAN, state))
    sent_rows = TILE + 8 + rows
    back_rows = TILE + rows

    sent = pl.pallas_call(
        state_kernel,
        name="device_state",
        out_shape=jax.ShapeDtypeStruct((count, sent_rows, TILE), F32),
        grid=(spans,),
        in_specs=[smem, head_spec, dt_spec, wide_spec, state_spec, whole((steps, seqs, state))],
        out_specs=whole((count, sent_rows, TILE)),
        scratch_shapes=[pltpu.VMEM((state, width), F32), pltpu.VMEM((heads, TILE), F32)],
        compiler_params=params(24),
        cost_estimate=pl.CostEstimate(
            flops=8 * length * state * width, bytes_accessed=6 * 2**20, transcendentals=0
        ),
    )(lengths, *map(in_hbm, (decay_rate, dt, x, b, dec_c)))
    owned = lax.all_to_all(sent, SEQ, 0, 0)

    parts = pl.pallas_call(
        local_kernel,
        name="device_outputs",
        out_shape=pltpu.HBM((2, length, width), F32),
        grid=(spans,),
        in_specs=[
            smem, head_spec, head_spec, dt_spec, wide_spec, wide_spec, state_spec, state_spec,
        ],
        out_specs=pair_spec,
        scratch_shapes=[
            pltpu.VMEM((state, width), F32),
            pltpu.VMEM((heads, TILE), F32),
            pltpu.VMEM((8, width), F32),
        ],
        compiler_params=params(32),
        cost_estimate=pl.CostEstimate(
            flops=20 * length * state * width, bytes_accessed=14 * 2**20, transcendentals=0
        ),
    )(lengths, *map(in_hbm, (decay_rate, skip_gain, dt, x, gate, b, c)))

    dec_part, dec_coef = pl.pallas_call(
        decode_kernel,
        name="decode_own",
        out_shape=[jax.ShapeDtypeStruct((rows, width), F32)] * 2,
        grid=(seqs,),
        in_specs=[
            smem, head_spec, head_spec, whole((steps, seqs, heads)),
            whole((steps, seqs, width)), whole((steps, seqs, width)),
            whole((steps, seqs, state)), whole((steps, seqs, state)),
            by_rows((1, width, state)),
        ],
        out_specs=[whole((rows, width))] * 2,
        scratch_shapes=[
            pltpu.VMEM((rows, width), F32), pltpu.VMEM((rows, width), F32),
            pltpu.VMEM((rows, state), F32), pltpu.VMEM((rows, state), F32),
            pltpu.VMEM((rows, heads), F32), pltpu.VMEM((rows, heads), F32),
        ],
        compiler_params=params(16),
        cost_estimate=pl.CostEstimate(
            flops=4 * seqs * 256 * state * width, bytes_accessed=5 * 2**20, transcendentals=0
        ),
    )(
        slots,
        *map(in_hbm, (decay_rate, skip_gain, dec_dt, dec_x, dec_gate, dec_b, dec_c)),
        in_hbm(dec_states.reshape(seqs, width, state)),
    )

    owned, parts, dec_part, dec_coef = lax.optimization_barrier(
        (owned, parts, dec_part, dec_coef)
    )
    back = pl.pallas_call(
        prefix_kernel,
        name="prefix",
        out_shape=jax.ShapeDtypeStruct((count, back_rows, TILE), F32),
        compiler_params=pltpu.CompilerParams(vmem_limit_bytes=16 * 2**20),
        cost_estimate=pl.CostEstimate(
            flops=2 * count * rows * TILE * TILE, bytes_accessed=3 * 2**20, transcendentals=0
        ),
    )(owned)
    entry = lax.all_to_all(back, SEQ, 0, 0)

    mixed, dec_mixed, power = pl.pallas_call(
        mix_kernel,
        name="mix",
        out_shape=[
            pltpu.VMEM((length, width), F32),
            jax.ShapeDtypeStruct((rows, width), F32),
            jax.ShapeDtypeStruct((8, SPAN), F32),
        ],
        grid=(spans,),
        in_specs=[
            whole((count, back_rows, TILE)), state_spec, pair_spec,
            whole((rows, width)), whole((rows, width)),
        ],
        out_specs=[wide_spec, whole((rows, width)), whole((8, SPAN))],
        scratch_shapes=[pltpu.VMEM((state, width), BF16), pltpu.VMEM((state, width), BF16)],
        compiler_params=params(40),
        cost_estimate=pl.CostEstimate(
            flops=4 * length * state * width, bytes_accessed=14 * 2**20, transcendentals=0
        ),
    )(entry, c, parts, dec_part, dec_coef)
    other = lax.ppermute(power, "pool", [(0, 1), (1, 0)])

    prefill_out, decode_out = pl.pallas_call(
        norm_kernel,
        name="norm",
        out_shape=[
            jax.ShapeDtypeStruct((length, width), BF16),
            jax.ShapeDtypeStruct((steps, seqs, width), BF16),
        ],
        grid=(spans,),
        in_specs=[
            whole((8, SPAN)), whole((8, SPAN)), whole((1, width)), wide_spec, whole((rows, width)),
        ],
        out_specs=[wide_spec, whole((steps, seqs, width))],
        scratch_shapes=[pltpu.VMEM((rows, width), F32)],
        compiler_params=params(16),
        cost_estimate=pl.CostEstimate(
            flops=4 * length * width, bytes_accessed=6 * 2**20, transcendentals=0
        ),
    )(power, other, norm_gain, mixed, dec_mixed)
    return (
        prefill_out.reshape(x_in.shape),
        decode_out.reshape(steps, seqs, 1, width),
    )


def solution(mesh):
    split = Mesh(
        mesh.devices.reshape(mesh.shape["pool"], 4, 4, mesh.shape["head"]),
        ("pool", "seq_0", "seq_1", "head"),
    )
    wide = P(None, SEQ, "head", "pool")
    shared = P(None, SEQ, "head", None)
    per_head = P("head", "pool")
    return jax.shard_map(
        shards,
        mesh=split,
        in_specs=(
            wide, wide, wide, shared, shared, P(), per_head, per_head, per_head,
            P(SEQ, "head", "pool", None, None), wide, wide, wide, shared, shared, P(SEQ),
        ),
        out_specs=(wide, wide),
        check_vma=False,
    )
```

```python
import jax
import jax.numpy as jnp
from jax import lax
from jax.experimental import pallas as pl
from jax.experimental.pallas import tpu as pltpu
from jax.sharding import Mesh
from jax.sharding import PartitionSpec as P

SEQ = ("seq_0", "seq_1")
HEAD_DIM = 64
SPAN = 256
TILE = 128
EPS = 1e-05
F32 = jnp.float32
BF16 = jnp.bfloat16


def iota(shape, dim):
    return lax.broadcasted_iota(jnp.int32, shape, dim)


def dot(a, b, ca, cb):
    return lax.dot_general(a, b, (((ca,), (cb,)), ((), ())), preferred_element_type=F32)


def exact_dot(a, b):
    return jnp.dot(a, b, precision=lax.Precision.HIGHEST, preferred_element_type=F32)


def split2(v):
    hi = v.astype(BF16)
    return hi, (v - hi.astype(F32)).astype(BF16)


def split3(v):
    hi = v.astype(BF16)
    rest = v - hi.astype(F32)
    mid = rest.astype(BF16)
    low = (rest - mid.astype(F32)).astype(BF16)
    return jnp.concatenate([hi, mid, low], axis=0)


def spread(heads, width):
    one = iota((heads, width), 0) == iota((heads, width), 1) // HEAD_DIM
    return jnp.where(one, 1.0, 0.0)


def spread3(heads, width):
    one = spread(heads, width).astype(BF16)
    return jnp.concatenate([one, one, one], axis=0)


def per_channel(v, table):
    return dot(split3(v), table, 0, 0)


def as_column(row):
    n = row.shape[1]
    return jnp.sum(jnp.where(iota((n, n), 0) == iota((n, n), 1), row, 0.0), axis=1, keepdims=True)


def as_row(column, width):
    n = column.shape[0]
    same = iota((n, width), 0) == iota((n, width), 1)
    return jnp.sum(jnp.where(same, column, 0.0), axis=0, keepdims=True)


def upper_ones(n):
    return jnp.where(iota((n, n), 0) <= iota((n, n), 1), 1.0, 0.0).astype(BF16)


def silu(v):
    return v * jax.nn.sigmoid(v)


def chosen(slots, steps):
    seqs = slots.shape[1]
    rows = steps * seqs
    seq = iota((1, rows), 1) % seqs
    takes, place = jnp.zeros((1, rows), jnp.int32), jnp.zeros((1, rows), jnp.int32)
    for d in range(seqs):
        continues = jnp.where(slots[:, d : d + 1] >= 0, 1, 0)
        takes = takes + jnp.where(seq == d, continues, 0)
        place = place + jnp.where(seq > d, continues, 0)
    shape = (steps * (seqs - 1), rows)
    row, col = iota(shape, 0), iota(shape, 1)
    same = (row % steps == col // seqs) & (row // steps == place) & (takes > 0)
    return jnp.where(same, 1.0, 0.0).astype(BF16)


def head_terms(dt_ref, rate, first, limit):
    heads, span = dt_ref.shape
    live = first + iota((heads, span), 1) < limit
    step = jnp.where(live, jax.nn.softplus(dt_ref[...].astype(F32)), 0.0)
    sums = dot(split3(-step * rate), upper_ones(span), 1, 0)
    return step, sums[:heads] + sums[heads : 2 * heads] + sums[2 * heads :]


def state_kernel(
    lengths_ref, rate_hbm, slots_hbm, dt_hbm, x_hbm, b_hbm, dec_c_hbm, out_hbm,
    rate_ref, slots_ref, dec_c_ref, dec_rows, dt, x, b, sent, sem_in, sem_out,
):
    heads, length = dt.shape
    chunks = 4
    halves = b.shape[1] // TILE
    wide = out_hbm.shape[0] // halves
    cols = x.shape[1] // chunks
    small = (
        (dt_hbm, dt), (rate_hbm, rate_ref), (dec_c_hbm, dec_c_ref), (slots_hbm, slots_ref),
        (b_hbm, b),
    )
    first = [pltpu.make_async_copy(*pair, sem_in.at[n]) for n, pair in enumerate(small)]
    loads = []
    for k in range(chunks):
        rows_at = pl.ds(k * (length // chunks), length // chunks)
        loads.append(pltpu.make_async_copy(x_hbm.at[rows_at, :], x.at[rows_at, :], sem_in.at[len(small) + k]))
    for load in (*first, *loads):
        load.start()
    for load in first[:2]:
        load.wait()
    limit = lengths_ref[0] - lax.axis_index(SEQ) * length
    live = iota((heads, length), 1) < limit
    step = jnp.where(live, jax.nn.softplus(dt[...].astype(F32)), 0.0)
    log = -step * as_column(rate_ref[...])
    spans = range(0, length, SPAN)
    stacked = jnp.concatenate([log[:, t : t + SPAN] for t in spans], axis=0)
    rows = stacked.shape[0]
    sums = dot(split3(stacked), upper_ones(SPAN), 1, 0)
    cum = sums[:rows] + sums[rows : 2 * rows] + sums[2 * rows :]
    rest = jnp.zeros((heads, 1), F32)
    weights = []
    for t in reversed(range(len(spans))):
        here = cum[t * heads : (t + 1) * heads]
        rest = rest + here[:, SPAN - 1 :]
        weights.append(step[:, t * SPAN : (t + 1) * SPAN] * jnp.exp(rest - here))
    weights = split3(jnp.concatenate(weights[::-1], axis=1))
    table = spread3(heads, chunks * cols)
    decay = per_channel(jnp.broadcast_to(jnp.exp(rest), (heads, TILE)), table)[:8]

    first[2].wait()
    first[3].wait()
    steps, seqs, _ = dec_c_ref.shape
    for s in range(steps):
        dec_rows[s * seqs : (s + 1) * seqs, :] = dec_c_ref[s].astype(F32)
    picked = dot(chosen(slots_ref[...], steps), dec_rows[...].astype(BF16), 1, 0)
    for half in range(halves):
        for col in range(wide):
            sent[half * wide + col, TILE + 8 :, :] = picked[:, half * TILE : (half + 1) * TILE]
    first[4].wait()
    b_twice = jnp.concatenate([b[...], b[...]], axis=0)
    spreads = [
        dot(weights, table[:, k * cols : (k + 1) * cols], 0, 0) for k in range(chunks)
    ]
    for load in loads:
        load.wait()
    stores = []
    for k in range(chunks):
        flow = x[:, k * cols : (k + 1) * cols].astype(F32) * spreads[k]
        state = dot(b_twice, jnp.concatenate(split2(flow), axis=0), 0, 0)
        for side in range(cols // TILE):
            col = k * (cols // TILE) + side
            for half in range(halves):
                j = half * wide + col
                at = slice(side * TILE, (side + 1) * TILE)
                sent[j, :TILE, :] = state[half * TILE : (half + 1) * TILE, at]
                sent[j, TILE : TILE + 8, :] = decay[:, col * TILE : (col + 1) * TILE]
                stores.append(pltpu.make_async_copy(sent.at[j], out_hbm.at[j], sem_out.at[j]))
                stores[-1].start()
    for store in stores:
        store.wait()


def prefix_kernel(in_ref, out_ref):
    count = in_ref.shape[0]
    dec = in_ref.shape[1] - TILE - 8
    state = jnp.zeros((TILE, TILE), F32)
    for k in range(count):
        out_ref[k, :TILE, :] = state
        state = state * in_ref[k, TILE : TILE + 1, :] + in_ref[k, :TILE, :]
    high, low = split2(state)
    c = in_ref[:, TILE + 8 :, :].reshape(count * dec, TILE).astype(BF16)
    y = dot(c, high, 1, 0) + dot(c, low, 1, 0)
    out_ref[:, TILE:, :] = y.reshape(count, dec, TILE)


def local_kernel(
    lengths_ref, rate_ref, skip_ref, dt_ref, x_ref, gate_ref, b_ref, c_ref,
    part_ref, coef_ref, state, total, skip,
):
    t = pl.program_id(0)
    heads, span = dt_ref.shape
    width = x_ref.shape[1]

    @pl.when(t == 0)
    def _():
        state[...] = jnp.zeros_like(state)
        total[...] = jnp.zeros_like(total)
        skip[...] = exact_dot(
            jnp.broadcast_to(skip_ref[...], (8, heads)), spread(heads, width)
        )

    table = spread3(heads, width)
    limit = lengths_ref[0] - lax.axis_index(SEQ) * (pl.num_programs(0) * span)
    step, cum = head_terms(dt_ref, as_column(rate_ref[...]), t * span, limit)
    last = cum[:, span - 1 :]
    b, c = b_ref[...], c_ref[...]
    x = x_ref[...].astype(F32)
    high, low = split2(x * per_channel(step * jnp.exp(-cum), table))
    lower = iota((span, span), 0) >= iota((span, span), 1)
    score_high, score_low = split2(jnp.where(lower, dot(c, b, 1, 1), 0.0))
    acc = dot(score_high, high, 1, 0) + dot(score_high, low, 1, 0) + dot(score_low, high, 1, 0)
    now = state[...]
    now_high, now_low = split2(now)
    acc = acc + dot(c, now_high, 1, 0) + dot(c, now_low, 1, 0)
    decay = per_channel(jnp.exp(cum), table)
    before = total[...]
    total[...] = before + last
    lane = iota((heads, TILE), 1)
    rows = per_channel(jnp.where(lane < 8, jnp.exp(last), jnp.exp(before)), table)
    live = t * span + iota((span, width), 0) < limit
    gate = jnp.where(live, silu(gate_ref[...].astype(F32)), 0.0)
    part_ref[...] = (acc * decay + skip[0:1] * x) * gate
    coef_ref[...] = decay * rows[8:9] * gate
    state[...] = (now + (dot(b, high, 0, 0) + dot(b, low, 0, 0))) * rows[0:1]


def decode_kernel(
    slots_ref, rate_ref, skip_ref, dt_ref, x_ref, gate_ref, b_ref, c_ref, state_ref,
    part_ref, coef_ref, x_all, gate_all, b_all, c_all, keep_log, size_all,
):
    d = pl.program_id(0)
    steps, seqs, width = x_ref.shape
    heads = dt_ref.shape[2]
    rows = steps * seqs

    @pl.when(d == 0)
    def _():
        total = jnp.zeros((seqs, heads), F32)
        for s in range(steps):
            at = pl.ds(s * seqs, seqs)
            size = jax.nn.softplus(dt_ref[s].astype(F32))
            total = total - size * rate_ref[...]
            keep_log[at, :] = total
            size_all[at, :] = size
            x_all[at, :] = x_ref[s].astype(F32)
            gate_all[at, :] = gate_ref[s].astype(F32)
            b_all[at, :] = b_ref[s].astype(F32)
            c_all[at, :] = c_ref[s].astype(F32)
        table = spread(heads, width)
        keep = exact_dot(jnp.exp(keep_log[...]), table)
        flow = exact_dot(size_all[...] * jnp.exp(-keep_log[...]), table) * x_all[...]
        scores = dot(c_all[...].astype(BF16), b_all[...].astype(BF16), 1, 1)
        row, col = iota((rows, rows), 0), iota((rows, rows), 1)
        same = (row % seqs == col % seqs) & (col <= row)
        inner = exact_dot(jnp.where(same, scores, 0.0), flow)
        skip = exact_dot(jnp.broadcast_to(skip_ref[...], (8, heads)), table)[0:1]
        gate = silu(gate_all[...])
        part_ref[...] = (keep * inner + skip * x_all[...]) * gate
        coef_ref[...] = keep * gate

    c = c_all[...].astype(BF16)
    high, low = split2(state_ref[0])
    own = dot(c, high, 1, 1) + dot(c, low, 1, 1)
    mine = iota((rows, 1), 0) % seqs == d
    take = mine & (slots_ref[d] < 0)
    part_ref[...] += jnp.where(take, own * coef_ref[...], 0.0)
    coef_ref[...] = jnp.where(take, 0.0, coef_ref[...])


def mix_kernel(
    coef_hbm, slots_ref, in_ref, c_ref, part_ref, dec_part_ref, dec_coef_ref,
    mixed_ref, dec_mixed_ref, power_ref, coef, sem,
):
    length, width = part_ref.shape
    loads = []
    for t in range(length // SPAN):
        at = pl.ds(t * SPAN, SPAN)
        loads.append(pltpu.make_async_copy(coef_hbm.at[at, :], coef.at[at, :], sem.at[t]))
        loads[-1].start()
    wide = width // TILE
    halves = in_ref.shape[0] // wide
    pieces = [
        jnp.concatenate([in_ref[h * wide + col, :TILE, :] for h in range(halves)], axis=0)
        for col in range(wide)
    ]
    twice = jnp.concatenate(split2(jnp.concatenate(pieces, axis=1)), axis=0)
    final = jnp.concatenate(
        [in_ref[col, TILE:, :] + in_ref[wide + col, TILE:, :] for col in range(wide)], axis=1
    )
    steps = final.shape[0] // (slots_ref.shape[1] - 1)
    picks = chosen(slots_ref[...], steps)
    final = dot(jnp.concatenate([picks] * 3, axis=0), split3(final), 0, 0)
    dec_mixed = dec_part_ref[...] + dec_coef_ref[...] * final
    dec_mixed_ref[...] = dec_mixed
    power = jnp.sum(dec_mixed * dec_mixed, axis=1, keepdims=True)
    power_ref[...] = jnp.zeros_like(power_ref)
    power_ref[4:5, :] = as_row(power, SPAN)
    for t in range(length // SPAN):
        at = slice(t * SPAN, (t + 1) * SPAN)
        c = c_ref[at, :]
        from_before = dot(jnp.concatenate([c, c], axis=1), twice, 1, 0)
        loads[t].wait()
        mixed = part_ref[at, :] + coef[at, :] * from_before
        mixed_ref[at, :] = mixed
        power_ref[t : t + 1, :] = as_row(jnp.sum(mixed * mixed, axis=1, keepdims=True), SPAN)


def norm_kernel(
    power_ref, other_ref, gain_ref, mixed_ref, dec_mixed_ref, out_hbm, dec_ref, out, dec, sem
):
    length, width = mixed_ref.shape
    scales = lax.rsqrt((power_ref[...] + other_ref[...]) / (2 * width) + EPS)
    stores = []
    for t in range(length // SPAN):
        at = pl.ds(t * SPAN, SPAN)
        out[at, :] = (mixed_ref[at, :] * as_column(scales[t : t + 1]) * gain_ref[...]).astype(BF16)
        stores.append(pltpu.make_async_copy(out.at[at, :], out_hbm.at[at, :], sem.at[t]))
        stores[-1].start()
    steps, seqs, _ = dec_ref.shape
    rows = steps * seqs
    dec[...] = dec_mixed_ref[...] * as_column(scales[4:5, :TILE])[:rows] * gain_ref[...]
    for s in range(steps):
        dec_ref[s] = dec[s * seqs : (s + 1) * seqs, :].astype(BF16)
    for store in stores:
        store.wait()


def params(mib):
    return pltpu.CompilerParams(
        dimension_semantics=("arbitrary",), vmem_limit_bytes=mib * 2**20
    )


def whole(shape):
    return pl.BlockSpec(shape, lambda t: (0,) * len(shape))


def by_rows(shape):
    return pl.BlockSpec(shape, lambda t: (t,) + (0,) * (len(shape) - 1))


def in_hbm(v):
    return pltpu.with_memory_space_constraint(v, pltpu.HBM)


def in_vmem(v):
    return pltpu.with_memory_space_constraint(v, pltpu.VMEM)


HBM = pl.BlockSpec(memory_space=pltpu.HBM)
VMEM = pl.BlockSpec(memory_space=pltpu.VMEM)
SMEM = pl.BlockSpec(memory_space=pltpu.SMEM)


def cost(flops, mib):
    return pl.CostEstimate(flops=flops, bytes_accessed=mib * 2**20, transcendentals=0)


def device_state(lengths, rate, slots, dt, x, b, dec_c, count):
    heads, length = dt.shape
    state, width = b.shape[1], x.shape[1]
    steps, seqs, _ = dec_c.shape
    shape = (count, TILE + 8 + steps * (seqs - 1), TILE)
    return pl.pallas_call(
        state_kernel,
        name="device_state",
        out_shape=pltpu.HBM(shape, F32),
        in_specs=[SMEM] + [HBM] * 6,
        out_specs=HBM,
        scratch_shapes=[
            pltpu.VMEM(rate.shape, F32),
            pltpu.VMEM(slots.shape, jnp.int32),
            pltpu.VMEM(dec_c.shape, BF16),
            pltpu.VMEM((steps * seqs, state), F32),
            pltpu.VMEM((heads, length), BF16),
            pltpu.VMEM((length, width), BF16),
            pltpu.VMEM((length, state), BF16),
            pltpu.VMEM(shape, F32),
            pltpu.SemaphoreType.DMA((9,)),
            pltpu.SemaphoreType.DMA((count,)),
        ],
        compiler_params=pltpu.CompilerParams(vmem_limit_bytes=48 * 2**20),
        cost_estimate=cost(8 * length * state * width, 6),
    )(lengths, *map(in_hbm, (rate, slots, dt, x, b, dec_c)))


def device_outputs(lengths, rate, skip, dt, x, gate, b, c):
    heads, length = dt.shape
    state, width = b.shape[1], x.shape[1]
    wide_spec, state_spec = by_rows((SPAN, width)), by_rows((SPAN, state))
    head_spec = whole((1, heads))
    return pl.pallas_call(
        local_kernel,
        name="device_outputs",
        out_shape=[pltpu.HBM((length, width), F32)] * 2,
        grid=(length // SPAN,),
        in_specs=[
            SMEM, head_spec, head_spec, pl.BlockSpec((heads, SPAN), lambda t: (0, t)),
            wide_spec, wide_spec, state_spec, state_spec,
        ],
        out_specs=[wide_spec, wide_spec],
        scratch_shapes=[
            pltpu.VMEM((state, width), F32),
            pltpu.VMEM((heads, TILE), F32),
            pltpu.VMEM((8, width), F32),
        ],
        compiler_params=params(32),
        cost_estimate=cost(20 * length * state * width, 14),
    )(lengths, *map(in_hbm, (rate, skip, dt, x, gate, b, c)))


def decode_own(slots, rate, skip, dt, x, gate, b, c, states):
    steps, seqs, width = x.shape
    heads, state, rows = dt.shape[2], b.shape[2], steps * seqs
    return pl.pallas_call(
        decode_kernel,
        name="decode_own",
        out_shape=[jax.ShapeDtypeStruct((rows, width), F32)] * 2,
        grid=(seqs,),
        in_specs=[
            SMEM, whole((1, heads)), whole((1, heads)), whole((steps, seqs, heads)),
            whole((steps, seqs, width)), whole((steps, seqs, width)),
            whole((steps, seqs, state)), whole((steps, seqs, state)),
            by_rows((1, width, state)),
        ],
        out_specs=[whole((rows, width))] * 2,
        scratch_shapes=[
            pltpu.VMEM((rows, width), F32), pltpu.VMEM((rows, width), F32),
            pltpu.VMEM((rows, state), F32), pltpu.VMEM((rows, state), F32),
            pltpu.VMEM((rows, heads), F32), pltpu.VMEM((rows, heads), F32),
        ],
        compiler_params=params(16),
        cost_estimate=cost(4 * seqs * 256 * state * width, 5),
    )(slots, *map(in_hbm, (rate, skip, dt, x, gate, b, c, states)))


def prefix(owned):
    count, rows, _ = owned.shape
    return pl.pallas_call(
        prefix_kernel,
        name="prefix",
        out_shape=jax.ShapeDtypeStruct((count, rows - 8, TILE), F32),
        compiler_params=pltpu.CompilerParams(vmem_limit_bytes=16 * 2**20),
        cost_estimate=cost(2 * count * 32 * TILE * TILE, 3),
    )(owned)


def mix(coef, slots, entry, c, part, dec_part, dec_coef):
    length, width = part.shape
    return pl.pallas_call(
        mix_kernel,
        name="mix",
        out_shape=[
            pltpu.VMEM((length, width), F32),
            pltpu.VMEM(dec_part.shape, F32),
            pltpu.VMEM((8, SPAN), F32),
        ],
        in_specs=[HBM] + [VMEM] * 6,
        out_specs=[VMEM] * 3,
        scratch_shapes=[
            pltpu.VMEM((length, width), F32), pltpu.SemaphoreType.DMA((length // SPAN,)),
        ],
        compiler_params=pltpu.CompilerParams(vmem_limit_bytes=32 * 2**20),
        cost_estimate=cost(4 * length * c.shape[1] * width, 14),
    )(in_hbm(coef), slots, entry, c, part, dec_part, dec_coef)


def norm(power, other, gain, mixed, dec_mixed, dec_shape):
    length, width = mixed.shape
    return pl.pallas_call(
        norm_kernel,
        name="norm",
        out_shape=[pltpu.HBM((length, width), BF16), jax.ShapeDtypeStruct(dec_shape, BF16)],
        in_specs=[VMEM] * 5,
        out_specs=[HBM, VMEM],
        scratch_shapes=[
            pltpu.VMEM((length, width), BF16),
            pltpu.VMEM(dec_mixed.shape, F32),
            pltpu.SemaphoreType.DMA((length // SPAN,)),
        ],
        compiler_params=pltpu.CompilerParams(vmem_limit_bytes=16 * 2**20),
        cost_estimate=cost(4 * length * width, 6),
    )(power, other, gain, mixed, dec_mixed)


def shards(
    x_in, gate_in, dt_raw, b_in, c_in, lengths, decay_rate, skip_gain, norm_gain,
    dec_states, dec_x, dec_gate, dec_dt, dec_b, dec_c, slots,
):
    _, length, _, width = x_in.shape
    heads, state = dt_raw.shape[3], b_in.shape[3]
    steps, seqs = dec_x.shape[:2]
    count = lax.axis_size(SEQ)
    x, gate = x_in.reshape(length, width), gate_in.reshape(length, width)
    dt = dt_raw.reshape(length, heads).T
    b, c = b_in.reshape(length, state), c_in.reshape(length, state)
    dec_x, dec_gate = dec_x.reshape(steps, seqs, width), dec_gate.reshape(steps, seqs, width)
    dec_b, dec_c = dec_b.reshape(steps, seqs, state), dec_c.reshape(steps, seqs, state)
    dec_dt = dec_dt.reshape(steps, seqs, heads)

    slots_row = slots.reshape(1, seqs)
    sent = device_state(lengths, decay_rate, slots_row, dt, x, b, dec_c, count)
    owned = lax.all_to_all(sent, SEQ, 0, 0)
    part, coef = device_outputs(lengths, decay_rate, skip_gain, dt, x, gate, b, c)
    dec_part, dec_coef = decode_own(
        slots, decay_rate, skip_gain, dec_dt, dec_x, dec_gate, dec_b, dec_c,
        dec_states.reshape(seqs, width, state),
    )
    owned, part, coef, dec_part, dec_coef = lax.optimization_barrier(
        (owned, part, coef, dec_part, dec_coef)
    )
    entry = lax.all_to_all(prefix(owned), SEQ, 0, 0)
    mixed, dec_mixed, power = mix(coef, slots_row, entry, c, part, dec_part, dec_coef)
    other = lax.ppermute(power, "pool", [(0, 1), (1, 0)])
    prefill_out, decode_out = norm(
        power, other, norm_gain, mixed, dec_mixed, (steps, seqs, width)
    )
    return prefill_out.reshape(x_in.shape), decode_out.reshape(steps, seqs, 1, width)


def solution(mesh):
    split = Mesh(
        mesh.devices.reshape(mesh.shape["pool"], 4, 4, mesh.shape["head"]),
        ("pool", "seq_0", "seq_1", "head"),
    )
    wide = P(None, SEQ, "head", "pool")
    shared = P(None, SEQ, "head", None)
    per_head = P("head", "pool")
    return jax.shard_map(
        shards,
        mesh=split,
        in_specs=(
            wide, wide, wide, shared, shared, P(), per_head, per_head, per_head,
            P(SEQ, "head", "pool", None, None), wide, wide, wide, shared, shared, P(SEQ),
        ),
        out_specs=(wide, wide),
        check_vma=False,
    )
```

```python
import functools

import jax
import jax.numpy as jnp
from jax import lax
from jax.experimental import pallas as pl
from jax.experimental.pallas import tpu as pltpu
from jax.sharding import Mesh
from jax.sharding import PartitionSpec as P

SEQ = ("seq_0", "seq_1")
HEAD_DIM = 64
SPAN = 256
TILE = 128
EPS = 1e-05
F32 = jnp.float32
BF16 = jnp.bfloat16


def iota(shape, dim):
    return lax.broadcasted_iota(jnp.int32, shape, dim)


def dot(a, b, ca, cb):
    return lax.dot_general(a, b, (((ca,), (cb,)), ((), ())), preferred_element_type=F32)


def exact_dot(a, b):
    return jnp.dot(a, b, precision=lax.Precision.HIGHEST, preferred_element_type=F32)


def split2(v):
    hi = v.astype(BF16)
    return hi, (v - hi.astype(F32)).astype(BF16)


def split3(v):
    hi = v.astype(BF16)
    rest = v - hi.astype(F32)
    mid = rest.astype(BF16)
    low = (rest - mid.astype(F32)).astype(BF16)
    return jnp.concatenate([hi, mid, low], axis=0)


def spread(heads, width):
    one = iota((heads, width), 0) == iota((heads, width), 1) // HEAD_DIM
    return jnp.where(one, 1.0, 0.0)


def spread3(heads, width):
    one = spread(heads, width).astype(BF16)
    return jnp.concatenate([one, one, one], axis=0)


def per_channel(v, table):
    return dot(split3(v), table, 0, 0)


def as_column(row):
    n = row.shape[1]
    return jnp.sum(jnp.where(iota((n, n), 0) == iota((n, n), 1), row, 0.0), axis=1, keepdims=True)


def as_row(column, width):
    n = column.shape[0]
    same = iota((n, width), 0) == iota((n, width), 1)
    return jnp.sum(jnp.where(same, column, 0.0), axis=0, keepdims=True)


def upper_ones(n):
    return jnp.where(iota((n, n), 0) <= iota((n, n), 1), 1.0, 0.0).astype(BF16)


def silu(v):
    return v * jax.nn.sigmoid(v)


def chosen(slots, steps):
    seqs = slots.shape[1]
    rows = steps * seqs
    seq = iota((1, rows), 1) % seqs
    takes, place = jnp.zeros((1, rows), jnp.int32), jnp.zeros((1, rows), jnp.int32)
    for d in range(seqs):
        continues = jnp.where(slots[:, d : d + 1] >= 0, 1, 0)
        takes = takes + jnp.where(seq == d, continues, 0)
        place = place + jnp.where(seq > d, continues, 0)
    shape = (steps * (seqs - 1), rows)
    row, col = iota(shape, 0), iota(shape, 1)
    same = (row % steps == col // seqs) & (row // steps == place) & (takes > 0)
    return jnp.where(same, 1.0, 0.0).astype(BF16)


def head_terms(dt_ref, rate, first, limit):
    heads, span = dt_ref.shape
    live = first + iota((heads, span), 1) < limit
    step = jnp.where(live, jax.nn.softplus(dt_ref[...].astype(F32)), 0.0)
    sums = dot(split3(-step * rate), upper_ones(span), 1, 0)
    return step, sums[:heads] + sums[heads : 2 * heads] + sums[2 * heads :]


def state_kernel(
    lengths_ref, rate_hbm, slots_hbm, dt_hbm, x_hbm, b_hbm, dec_c_hbm, _, out_hbm,
    rate_ref, slots_ref, dec_c_ref, dec_rows, dt, x, b, sent, sem_in, sem_out,
):
    heads, length = dt.shape
    chunks = 4
    halves = b.shape[1] // TILE
    wide = out_hbm.shape[0] // halves
    cols = x.shape[1] // chunks
    small = (
        (dt_hbm, dt), (rate_hbm, rate_ref), (dec_c_hbm, dec_c_ref), (slots_hbm, slots_ref),
        (b_hbm, b),
    )
    first = [pltpu.make_async_copy(*pair, sem_in.at[n]) for n, pair in enumerate(small)]
    loads = []
    for k in range(chunks):
        rows_at = pl.ds(k * (length // chunks), length // chunks)
        loads.append(pltpu.make_async_copy(x_hbm.at[rows_at, :], x.at[rows_at, :], sem_in.at[len(small) + k]))
    for load in (*first, *loads):
        load.start()
    for load in first[:2]:
        load.wait()
    limit = lengths_ref[0] - lax.axis_index(SEQ) * length
    live = iota((heads, length), 1) < limit
    step = jnp.where(live, jax.nn.softplus(dt[...].astype(F32)), 0.0)
    log = -step * as_column(rate_ref[...])
    spans = range(0, length, SPAN)
    stacked = jnp.concatenate([log[:, t : t + SPAN] for t in spans], axis=0)
    rows = stacked.shape[0]
    sums = dot(split3(stacked), upper_ones(SPAN), 1, 0)
    cum = sums[:rows] + sums[rows : 2 * rows] + sums[2 * rows :]
    rest = jnp.zeros((heads, 1), F32)
    weights = []
    for t in reversed(range(len(spans))):
        here = cum[t * heads : (t + 1) * heads]
        rest = rest + here[:, SPAN - 1 :]
        weights.append(step[:, t * SPAN : (t + 1) * SPAN] * jnp.exp(rest - here))
    weights = split3(jnp.concatenate(weights[::-1], axis=1))
    table = spread3(heads, chunks * cols)
    decay = per_channel(jnp.broadcast_to(jnp.exp(rest), (heads, TILE)), table)[:8]

    spreads = [
        dot(weights, table[:, k * cols : (k + 1) * cols], 0, 0) for k in range(chunks)
    ]
    for load in (*first[2:], *loads):
        load.wait()
    steps, seqs, _ = dec_c_ref.shape
    for s in range(steps):
        dec_rows[s * seqs : (s + 1) * seqs, :] = dec_c_ref[s].astype(F32)
    picked = dot(chosen(slots_ref[...], steps), dec_rows[...].astype(BF16), 1, 0)
    for half in range(halves):
        for col in range(wide):
            sent[half * wide + col, TILE + 8 :, :] = picked[:, half * TILE : (half + 1) * TILE]
    b_twice = jnp.concatenate([b[...], b[...]], axis=0)
    stores = []
    for k in range(chunks):
        flow = x[:, k * cols : (k + 1) * cols].astype(F32) * spreads[k]
        state = dot(b_twice, jnp.concatenate(split2(flow), axis=0), 0, 0)
        for side in range(cols // TILE):
            col = k * (cols // TILE) + side
            for half in range(halves):
                j = half * wide + col
                at = slice(side * TILE, (side + 1) * TILE)
                sent[j, :TILE, :] = state[half * TILE : (half + 1) * TILE, at]
                sent[j, TILE : TILE + 8, :] = decay[:, col * TILE : (col + 1) * TILE]
                stores.append(pltpu.make_async_copy(sent.at[j], out_hbm.at[j], sem_out.at[j]))
                stores[-1].start()
    for store in stores:
        store.wait()


def prefix_kernel(in_ref, out_ref):
    count = in_ref.shape[0]
    dec = in_ref.shape[1] - TILE - 8
    state = jnp.zeros((TILE, TILE), F32)
    for k in range(count):
        out_ref[k, :TILE, :] = state
        state = state * in_ref[k, TILE : TILE + 1, :] + in_ref[k, :TILE, :]
    high, low = split2(state)
    c = in_ref[:, TILE + 8 :, :].reshape(count * dec, TILE).astype(BF16)
    y = dot(c, high, 1, 0) + dot(c, low, 1, 0)
    out_ref[:, TILE:, :] = y.reshape(count, dec, TILE)


def local_kernel(
    lengths_ref, rate_ref, skip_ref, dt_ref, x_ref, gate_ref, b_ref, c_ref,
    part_ref, coef_ref, state, total, skip,
):
    t = pl.program_id(0)
    heads, span = dt_ref.shape
    width = x_ref.shape[1]

    @pl.when(t == 0)
    def _():
        state[...] = jnp.zeros_like(state)
        total[...] = jnp.zeros_like(total)
        skip[...] = exact_dot(
            jnp.broadcast_to(skip_ref[...], (8, heads)), spread(heads, width)
        )

    table = spread3(heads, width)
    limit = lengths_ref[0] - lax.axis_index(SEQ) * (pl.num_programs(0) * span)
    step, cum = head_terms(dt_ref, as_column(rate_ref[...]), t * span, limit)
    last = cum[:, span - 1 :]
    b, c = b_ref[...], c_ref[...]
    x = x_ref[...].astype(F32)
    high, low = split2(x * per_channel(step * jnp.exp(-cum), table))
    lower = iota((span, span), 0) >= iota((span, span), 1)
    score_high, score_low = split2(jnp.where(lower, dot(c, b, 1, 1), 0.0))
    acc = dot(score_high, high, 1, 0) + dot(score_high, low, 1, 0) + dot(score_low, high, 1, 0)
    now = state[...]
    now_high, now_low = split2(now)
    acc = acc + dot(c, now_high, 1, 0) + dot(c, now_low, 1, 0)
    decay = per_channel(jnp.exp(cum), table)
    before = total[...]
    total[...] = before + last
    lane = iota((heads, TILE), 1)
    rows = per_channel(jnp.where(lane < 8, jnp.exp(last), jnp.exp(before)), table)
    live = t * span + iota((span, width), 0) < limit
    gate = jnp.where(live, silu(gate_ref[...].astype(F32)), 0.0)
    part_ref[...] = (acc * decay + skip[0:1] * x) * gate
    coef_ref[...] = decay * rows[8:9] * gate
    state[...] = (now + (dot(b, high, 0, 0) + dot(b, low, 0, 0))) * rows[0:1]


def decode_kernel(turn, *refs):
    part_hbm, coef_hbm = refs[9:11]
    work, (part, coef, sem), store_sem = refs[11:-4], refs[-4:-1], refs[-1]

    @pl.when(lax.axis_index("pool") == turn)
    def _():
        decode_work(*refs[:9], *work, part, coef, sem)
        pairs = ((part, part_hbm), (coef, coef_hbm))
        stores = [pltpu.make_async_copy(*p, store_sem.at[n]) for n, p in enumerate(pairs)]
        for store in stores:
            store.start()
        for store in stores:
            store.wait()


def decode_work(
    slots_hbm, rate_hbm, skip_hbm, dt_hbm, x_hbm, gate_hbm, b_hbm, c_hbm, states_hbm,
    slots_ref, rate_ref, skip_ref, dt_ref, x_ref, gate_ref, b_ref, c_ref, states,
    x_all, gate_all, b_all, c_all, keep_log, size_all, part, coef, sem,
):
    steps, seqs, width = x_ref.shape
    heads = dt_ref.shape[2]
    rows = steps * seqs
    pairs = (
        (slots_hbm, slots_ref), (rate_hbm, rate_ref), (skip_hbm, skip_ref), (dt_hbm, dt_ref),
        (x_hbm, x_ref), (gate_hbm, gate_ref), (b_hbm, b_ref), (c_hbm, c_ref),
        (states_hbm, states),
    )
    loads = [pltpu.make_async_copy(*pair, sem.at[n]) for n, pair in enumerate(pairs)]
    for load in loads:
        load.start()
    for load in loads[:-1]:
        load.wait()
    total = jnp.zeros((seqs, heads), F32)
    for s in range(steps):
        at = pl.ds(s * seqs, seqs)
        size = jax.nn.softplus(dt_ref[s].astype(F32))
        total = total - size * rate_ref[...]
        keep_log[at, :] = total
        size_all[at, :] = size
        x_all[at, :] = x_ref[s].astype(F32)
        gate_all[at, :] = gate_ref[s].astype(F32)
        b_all[at, :] = b_ref[s].astype(F32)
        c_all[at, :] = c_ref[s].astype(F32)
    table = spread(heads, width)
    keep = exact_dot(jnp.exp(keep_log[...]), table)
    flow = exact_dot(size_all[...] * jnp.exp(-keep_log[...]), table) * x_all[...]
    c = c_all[...].astype(BF16)
    scores = dot(c, b_all[...].astype(BF16), 1, 1)
    row, col = iota((rows, rows), 0), iota((rows, rows), 1)
    same = (row % seqs == col % seqs) & (col <= row)
    inner = exact_dot(jnp.where(same, scores, 0.0), flow)
    skip = exact_dot(jnp.broadcast_to(skip_ref[...], (8, heads)), table)[0:1]
    gate = silu(gate_all[...])
    seq = iota((rows, 1), 0) % seqs
    loads[-1].wait()
    own = jnp.zeros((rows, width), F32)
    keeps = jnp.zeros((rows, 1), jnp.int32)
    for d in range(seqs):
        high, low = split2(states[d])
        mine = (seq == d) & (slots_ref[:, d : d + 1] < 0)
        own = jnp.where(mine, dot(c, high, 1, 1) + dot(c, low, 1, 1), own)
        keeps = jnp.where(mine, 1, keeps)
    part[...] = (keep * (inner + own) + skip * x_all[...]) * gate
    coef[...] = jnp.where(keeps > 0, 0.0, keep * gate)


def mix_kernel(turn, *refs):
    decode, refs = refs[:9], refs[9:]
    coef_hbm, dec_part_hbm, dec_coef_hbm, slots_ref, in_ref, c_ref, part_ref = refs[:7]
    mixed_ref, dec_mixed_ref, power_ref, coef, sem, *work = refs[7:]
    dec_part, dec_coef = work[-3:-1]
    length, width = part_ref.shape
    loads = []
    for t in range(length // SPAN):
        at = pl.ds(t * SPAN, SPAN)
        loads.append(pltpu.make_async_copy(coef_hbm.at[at, :], coef.at[at, :], sem.at[t]))
        loads[-1].start()
    pairs = ((dec_part_hbm, dec_part), (dec_coef_hbm, dec_coef))
    done = [pltpu.make_async_copy(*p, sem.at[len(loads) + n]) for n, p in enumerate(pairs)]

    @pl.when(lax.axis_index("pool") != turn)
    def _():
        for load in done:
            load.start()

    wide = width // TILE
    halves = in_ref.shape[0] // wide
    pieces = [
        jnp.concatenate([in_ref[h * wide + col, :TILE, :] for h in range(halves)], axis=0)
        for col in range(wide)
    ]
    twice = jnp.concatenate(split2(jnp.concatenate(pieces, axis=1)), axis=0)
    power_ref[...] = jnp.zeros_like(power_ref)
    spans = length // SPAN

    def carried(t):
        c = c_ref[t * SPAN : (t + 1) * SPAN, :]
        return dot(jnp.concatenate([c, c], axis=1), twice, 1, 0)

    each = spans // 2
    ready = [carried(t) for t in range(each)]
    for k in range(2):
        now = ready
        for load in loads[k * each : (k + 1) * each]:
            load.wait()
        if k + 1 < 2:
            ready = [carried(t) for t in range((k + 1) * each, (k + 2) * each)]
        for t in range(k * each, (k + 1) * each):
            at = slice(t * SPAN, (t + 1) * SPAN)
            mixed = part_ref[at, :] + coef[at, :] * now[t - k * each]
            mixed_ref[at, :] = mixed
            power_ref[t : t + 1, :] = as_row(jnp.sum(mixed * mixed, axis=1, keepdims=True), SPAN)

    @pl.when(lax.axis_index("pool") != turn)
    def _():
        for load in done:
            load.wait()

    @pl.when(lax.axis_index("pool") == turn)
    def _():
        decode_work(*decode, *work)

    final = jnp.concatenate(
        [in_ref[col, TILE:, :] + in_ref[wide + col, TILE:, :] for col in range(wide)], axis=1
    )
    steps = final.shape[0] // (slots_ref.shape[1] - 1)
    picks = chosen(slots_ref[...], steps)
    final = dot(jnp.concatenate([picks] * 3, axis=0), split3(final), 0, 0)
    dec_mixed = dec_part[...] + dec_coef[...] * final
    dec_mixed_ref[...] = dec_mixed
    power = jnp.sum(dec_mixed * dec_mixed, axis=1, keepdims=True)
    power_ref[4:5, :] = as_row(power, SPAN)


def norm_kernel(
    power_ref, other_ref, gain_ref, mixed_ref, dec_mixed_ref, out_hbm, dec_ref, out, dec, sem
):
    length, width = mixed_ref.shape
    scales = lax.rsqrt((power_ref[...] + other_ref[...]) / (2 * width) + EPS)
    stores = []
    for t in range(length // SPAN):
        at = pl.ds(t * SPAN, SPAN)
        out[at, :] = (mixed_ref[at, :] * as_column(scales[t : t + 1]) * gain_ref[...]).astype(BF16)
        stores.append(pltpu.make_async_copy(out.at[at, :], out_hbm.at[at, :], sem.at[t]))
        stores[-1].start()
    steps, seqs, _ = dec_ref.shape
    rows = steps * seqs
    dec[...] = dec_mixed_ref[...] * as_column(scales[4:5, :TILE])[:rows] * gain_ref[...]
    for s in range(steps):
        dec_ref[s] = dec[s * seqs : (s + 1) * seqs, :].astype(BF16)
    for store in stores:
        store.wait()


def params(mib):
    return pltpu.CompilerParams(
        dimension_semantics=("arbitrary",), vmem_limit_bytes=mib * 2**20
    )


def whole(shape):
    return pl.BlockSpec(shape, lambda t: (0,) * len(shape))


def by_rows(shape):
    return pl.BlockSpec(shape, lambda t: (t,) + (0,) * (len(shape) - 1))


def in_hbm(v):
    return pltpu.with_memory_space_constraint(v, pltpu.HBM)


def in_vmem(v):
    return pltpu.with_memory_space_constraint(v, pltpu.VMEM)


HBM = pl.BlockSpec(memory_space=pltpu.HBM)
VMEM = pl.BlockSpec(memory_space=pltpu.VMEM)
SMEM = pl.BlockSpec(memory_space=pltpu.SMEM)


def cost(flops, mib):
    return pl.CostEstimate(flops=flops, bytes_accessed=mib * 2**20, transcendentals=0)


def device_state(lengths, rate, slots, dt, x, b, dec_c, after, count):
    heads, length = dt.shape
    state, width = b.shape[1], x.shape[1]
    steps, seqs, _ = dec_c.shape
    shape = (count, TILE + 8 + steps * (seqs - 1), TILE)
    return pl.pallas_call(
        state_kernel,
        name="device_state",
        out_shape=pltpu.HBM(shape, F32),
        in_specs=[SMEM] + [HBM] * 7,
        out_specs=HBM,
        scratch_shapes=[
            pltpu.VMEM(rate.shape, F32),
            pltpu.VMEM(slots.shape, jnp.int32),
            pltpu.VMEM(dec_c.shape, BF16),
            pltpu.VMEM((steps * seqs, state), F32),
            pltpu.VMEM((heads, length), BF16),
            pltpu.VMEM((length, width), BF16),
            pltpu.VMEM((length, state), BF16),
            pltpu.VMEM(shape, F32),
            pltpu.SemaphoreType.DMA((9,)),
            pltpu.SemaphoreType.DMA((count,)),
        ],
        compiler_params=pltpu.CompilerParams(vmem_limit_bytes=48 * 2**20),
        cost_estimate=cost(8 * length * state * width, 6),
    )(lengths, *map(in_hbm, (rate, slots, dt, x, b, dec_c, after)))


def device_outputs(lengths, rate, skip, dt, x, gate, b, c):
    heads, length = dt.shape
    state, width = b.shape[1], x.shape[1]
    wide_spec, state_spec = by_rows((SPAN, width)), by_rows((SPAN, state))
    head_spec = whole((1, heads))
    return pl.pallas_call(
        local_kernel,
        name="device_outputs",
        out_shape=[pltpu.HBM((length, width), F32)] * 2,
        grid=(length // SPAN,),
        in_specs=[
            SMEM, head_spec, head_spec, pl.BlockSpec((heads, SPAN), lambda t: (0, t)),
            wide_spec, wide_spec, state_spec, state_spec,
        ],
        out_specs=[wide_spec, wide_spec],
        scratch_shapes=[
            pltpu.VMEM((state, width), F32),
            pltpu.VMEM((heads, TILE), F32),
            pltpu.VMEM((8, width), F32),
        ],
        compiler_params=params(32),
        cost_estimate=cost(20 * length * state * width, 14),
    )(lengths, *map(in_hbm, (rate, skip, dt, x, gate, b, c)))


def decode_scratch(arrays):
    steps, seqs, width = arrays[4].shape
    rows, state, heads = steps * seqs, arrays[6].shape[2], arrays[3].shape[2]
    wide, narrow, small = (pltpu.VMEM((rows, n), F32) for n in (width, state, heads))
    return [
        *(pltpu.VMEM(a.shape, a.dtype) for a in arrays),
        wide, wide, narrow, narrow, small, small, wide, wide,
        pltpu.SemaphoreType.DMA((len(arrays),)),
    ]


def decode_own(turn, arrays):
    steps, seqs, width = arrays[4].shape
    state, rows = arrays[6].shape[2], steps * seqs
    return pl.pallas_call(
        functools.partial(decode_kernel, turn),
        name="decode_own",
        out_shape=[pltpu.HBM((rows, width), F32)] * 2,
        in_specs=[HBM] * len(arrays),
        out_specs=[HBM] * 2,
        scratch_shapes=[*decode_scratch(arrays), pltpu.SemaphoreType.DMA((2,))],
        compiler_params=pltpu.CompilerParams(vmem_limit_bytes=32 * 2**20),
        cost_estimate=cost(4 * seqs * 256 * state * width, 5),
    )(*map(in_hbm, arrays))


def prefix(owned):
    count, rows, _ = owned.shape
    return pl.pallas_call(
        prefix_kernel,
        name="prefix",
        out_shape=jax.ShapeDtypeStruct((count, rows - 8, TILE), F32),
        compiler_params=pltpu.CompilerParams(vmem_limit_bytes=16 * 2**20),
        cost_estimate=cost(2 * count * 32 * TILE * TILE, 3),
    )(owned)


def mix(turn, decode, coef, dec_part, dec_coef, slots, entry, c, part):
    length, width = part.shape
    return pl.pallas_call(
        functools.partial(mix_kernel, turn),
        name="mix",
        out_shape=[
            pltpu.VMEM((length, width), F32),
            pltpu.VMEM(dec_part.shape, F32),
            pltpu.VMEM((8, SPAN), F32),
        ],
        in_specs=[HBM] * 12 + [VMEM] * 4,
        out_specs=[VMEM] * 3,
        scratch_shapes=[
            pltpu.VMEM((length, width), F32),
            pltpu.SemaphoreType.DMA((length // SPAN + 2,)),
            *decode_scratch(decode),
        ],
        compiler_params=pltpu.CompilerParams(vmem_limit_bytes=40 * 2**20),
        cost_estimate=cost(4 * length * c.shape[1] * width, 14),
    )(*map(in_hbm, (*decode, coef, dec_part, dec_coef)), slots, entry, c, part)


def norm(power, other, gain, mixed, dec_mixed, dec_shape):
    length, width = mixed.shape
    return pl.pallas_call(
        norm_kernel,
        name="norm",
        out_shape=[pltpu.HBM((length, width), BF16), jax.ShapeDtypeStruct(dec_shape, BF16)],
        in_specs=[VMEM] * 5,
        out_specs=[HBM, VMEM],
        scratch_shapes=[
            pltpu.VMEM((length, width), BF16),
            pltpu.VMEM(dec_mixed.shape, F32),
            pltpu.SemaphoreType.DMA((length // SPAN,)),
        ],
        compiler_params=pltpu.CompilerParams(vmem_limit_bytes=16 * 2**20),
        cost_estimate=cost(4 * length * width, 6),
    )(power, other, gain, mixed, dec_mixed)


def shards(
    x_in, gate_in, dt_raw, b_in, c_in, lengths, decay_rate, skip_gain, norm_gain,
    dec_states, dec_x, dec_gate, dec_dt, dec_b, dec_c, slots,
):
    _, length, _, width = x_in.shape
    heads, state = dt_raw.shape[3], b_in.shape[3]
    steps, seqs = dec_x.shape[:2]
    count = lax.axis_size(SEQ)
    x, gate = x_in.reshape(length, width), gate_in.reshape(length, width)
    dt = dt_raw.reshape(length, heads).T
    b, c = b_in.reshape(length, state), c_in.reshape(length, state)
    dec_x, dec_gate = dec_x.reshape(steps, seqs, width), dec_gate.reshape(steps, seqs, width)
    dec_b, dec_c = dec_b.reshape(steps, seqs, state), dec_c.reshape(steps, seqs, state)
    dec_dt = dec_dt.reshape(steps, seqs, heads)

    slots_row = slots.reshape(1, seqs)
    decode = (
        slots_row, decay_rate, skip_gain, dec_dt, dec_x, dec_gate, dec_b, dec_c,
        dec_states.reshape(seqs, width, state),
    )
    dec_part, dec_coef = decode_own(0, decode)
    sent = device_state(lengths, decay_rate, slots_row, dt, x, b, dec_c, dec_part, count)
    owned = lax.all_to_all(sent, SEQ, 0, 0)
    part, coef = device_outputs(lengths, decay_rate, skip_gain, dt, x, gate, b, c)
    owned, part, coef = lax.optimization_barrier((owned, part, coef))
    entry = lax.all_to_all(prefix(owned), SEQ, 0, 0)
    mixed, dec_mixed, power = mix(
        1, decode, coef, dec_part, dec_coef, slots_row, entry, c, part
    )
    other = lax.ppermute(power, "pool", [(0, 1), (1, 0)])
    prefill_out, decode_out = norm(
        power, other, norm_gain, mixed, dec_mixed, (steps, seqs, width)
    )
    return prefill_out.reshape(x_in.shape), decode_out.reshape(steps, seqs, 1, width)


def solution(mesh):
    split = Mesh(
        mesh.devices.reshape(mesh.shape["pool"], 4, 4, mesh.shape["head"]),
        ("pool", "seq_0", "seq_1", "head"),
    )
    wide = P(None, SEQ, "head", "pool")
    shared = P(None, SEQ, "head", None)
    per_head = P("head", "pool")
    return jax.shard_map(
        shards,
        mesh=split,
        in_specs=(
            wide, wide, wide, shared, shared, P(), per_head, per_head, per_head,
            P(SEQ, "head", "pool", None, None), wide, wide, wide, shared, shared, P(SEQ),
        ),
        out_specs=(wide, wide),
        check_vma=False,
    )
```

```python
import functools

import jax
import jax.numpy as jnp
from jax import lax
from jax.experimental import pallas as pl
from jax.experimental.pallas import tpu as pltpu
from jax.sharding import Mesh
from jax.sharding import PartitionSpec as P

SEQ = ("seq_0", "seq_1")
HEAD_DIM = 64
SPAN = 256
TILE = 128
EPS = 1e-05
F32 = jnp.float32
BF16 = jnp.bfloat16


def iota(shape, dim):
    return lax.broadcasted_iota(jnp.int32, shape, dim)


def dot(a, b, ca, cb):
    return lax.dot_general(a, b, (((ca,), (cb,)), ((), ())), preferred_element_type=F32)


def exact_dot(a, b):
    return jnp.dot(a, b, precision=lax.Precision.HIGHEST, preferred_element_type=F32)


def split2(v):
    hi = v.astype(BF16)
    return hi, (v - hi.astype(F32)).astype(BF16)


def split3(v):
    hi = v.astype(BF16)
    rest = v - hi.astype(F32)
    mid = rest.astype(BF16)
    low = (rest - mid.astype(F32)).astype(BF16)
    return jnp.concatenate([hi, mid, low], axis=0)


def spread(heads, width):
    one = iota((heads, width), 0) == iota((heads, width), 1) // HEAD_DIM
    return jnp.where(one, 1.0, 0.0)


def spread3(heads, width):
    one = spread(heads, width).astype(BF16)
    return jnp.concatenate([one, one, one], axis=0)


def per_channel(v, table):
    return dot(split3(v), table, 0, 0)


def as_column(row):
    n = row.shape[1]
    return jnp.sum(jnp.where(iota((n, n), 0) == iota((n, n), 1), row, 0.0), axis=1, keepdims=True)


def as_row(column, width):
    n = column.shape[0]
    same = iota((n, width), 0) == iota((n, width), 1)
    return jnp.sum(jnp.where(same, column, 0.0), axis=0, keepdims=True)


def upper_ones(n):
    return jnp.where(iota((n, n), 0) <= iota((n, n), 1), 1.0, 0.0).astype(BF16)


def silu(v):
    return v * jax.nn.sigmoid(v)


def chosen(slots, steps):
    seqs = slots.shape[1]
    rows = steps * seqs
    seq = iota((1, rows), 1) % seqs
    takes, place = jnp.zeros((1, rows), jnp.int32), jnp.zeros((1, rows), jnp.int32)
    for d in range(seqs):
        continues = jnp.where(slots[:, d : d + 1] >= 0, 1, 0)
        takes = takes + jnp.where(seq == d, continues, 0)
        place = place + jnp.where(seq > d, continues, 0)
    shape = (steps * (seqs - 1), rows)
    row, col = iota(shape, 0), iota(shape, 1)
    same = (row % steps == col // seqs) & (row // steps == place) & (takes > 0)
    return jnp.where(same, 1.0, 0.0).astype(BF16)


def head_terms(dt_ref, rate, first, limit):
    heads, span = dt_ref.shape
    live = first + iota((heads, span), 1) < limit
    step = jnp.where(live, jax.nn.softplus(dt_ref[...].astype(F32)), 0.0)
    sums = dot(split3(-step * rate), upper_ones(span), 1, 0)
    return step, sums[:heads] + sums[heads : 2 * heads] + sums[2 * heads :]


def state_kernel(
    lengths_ref, rate_hbm, slots_hbm, dt_hbm, x_hbm, b_hbm, dec_c_hbm, _, out_hbm,
    rate_ref, slots_ref, dec_c_ref, dec_rows, dt, x, b, sent, sem_in, sem_out,
):
    heads, length = dt.shape
    chunks = 4
    halves = b.shape[1] // TILE
    wide = out_hbm.shape[0] // halves
    cols = x.shape[1] // chunks
    small = (
        (dt_hbm, dt), (rate_hbm, rate_ref), (dec_c_hbm, dec_c_ref), (slots_hbm, slots_ref),
        (b_hbm, b),
    )
    first = [pltpu.make_async_copy(*pair, sem_in.at[n]) for n, pair in enumerate(small)]
    loads = []
    for k in range(chunks):
        rows_at = pl.ds(k * (length // chunks), length // chunks)
        loads.append(pltpu.make_async_copy(x_hbm.at[rows_at, :], x.at[rows_at, :], sem_in.at[len(small) + k]))
    for load in (*first, *loads):
        load.start()
    for load in first[:2]:
        load.wait()
    limit = lengths_ref[0] - lax.axis_index(SEQ) * length
    live = iota((heads, length), 1) < limit
    step = jnp.where(live, jax.nn.softplus(dt[...].astype(F32)), 0.0)
    log = -step * as_column(rate_ref[...])
    spans = range(0, length, SPAN)
    stacked = jnp.concatenate([log[:, t : t + SPAN] for t in spans], axis=0)
    rows = stacked.shape[0]
    sums = dot(split3(stacked), upper_ones(SPAN), 1, 0)
    cum = sums[:rows] + sums[rows : 2 * rows] + sums[2 * rows :]
    rest = jnp.zeros((heads, 1), F32)
    weights = []
    for t in reversed(range(len(spans))):
        here = cum[t * heads : (t + 1) * heads]
        rest = rest + here[:, SPAN - 1 :]
        weights.append(step[:, t * SPAN : (t + 1) * SPAN] * jnp.exp(rest - here))
    weights = split3(jnp.concatenate(weights[::-1], axis=1))
    table = spread3(heads, chunks * cols)
    decay = per_channel(jnp.broadcast_to(jnp.exp(rest), (heads, TILE)), table)[:8]

    spreads = [
        dot(weights, table[:, k * cols : (k + 1) * cols], 0, 0) for k in range(chunks)
    ]
    for load in (*first[2:], *loads):
        load.wait()
    steps, seqs, _ = dec_c_ref.shape
    for s in range(steps):
        dec_rows[s * seqs : (s + 1) * seqs, :] = dec_c_ref[s].astype(F32)
    picked = dot(chosen(slots_ref[...], steps), dec_rows[...].astype(BF16), 1, 0)
    for half in range(halves):
        for col in range(wide):
            sent[half * wide + col, TILE + 8 :, :] = picked[:, half * TILE : (half + 1) * TILE]
    b_twice = jnp.concatenate([b[...], b[...]], axis=0)
    stores = []
    for k in range(chunks):
        flow = x[:, k * cols : (k + 1) * cols].astype(F32) * spreads[k]
        state = dot(b_twice, jnp.concatenate(split2(flow), axis=0), 0, 0)
        for side in range(cols // TILE):
            col = k * (cols // TILE) + side
            for half in range(halves):
                j = half * wide + col
                at = slice(side * TILE, (side + 1) * TILE)
                sent[j, :TILE, :] = state[half * TILE : (half + 1) * TILE, at]
                sent[j, TILE : TILE + 8, :] = decay[:, col * TILE : (col + 1) * TILE]
                stores.append(pltpu.make_async_copy(sent.at[j], out_hbm.at[j], sem_out.at[j]))
                stores[-1].start()
    for store in stores:
        store.wait()


def prefix_kernel(in_ref, out_ref):
    count = in_ref.shape[0]
    dec = in_ref.shape[1] - TILE - 8
    state = jnp.zeros((TILE, TILE), F32)
    for k in range(count):
        out_ref[k, :TILE, :] = state
        state = state * in_ref[k, TILE : TILE + 1, :] + in_ref[k, :TILE, :]
    high, low = split2(state)
    c = in_ref[:, TILE + 8 :, :].reshape(count * dec, TILE).astype(BF16)
    y = dot(c, high, 1, 0) + dot(c, low, 1, 0)
    out_ref[:, TILE:, :] = y.reshape(count, dec, TILE)


def local_kernel(
    lengths_ref, rate_ref, skip_ref, dt_ref, x_ref, gate_ref, b_ref, c_ref,
    part_ref, coef_ref, state, total, skip,
):
    t = pl.program_id(0)
    heads, span = dt_ref.shape
    width = x_ref.shape[1]

    @pl.when(t == 0)
    def _():
        state[...] = jnp.zeros_like(state)
        total[...] = jnp.zeros_like(total)
        skip[...] = exact_dot(
            jnp.broadcast_to(skip_ref[...], (8, heads)), spread(heads, width)
        )

    table = spread3(heads, width)
    limit = lengths_ref[0] - lax.axis_index(SEQ) * (pl.num_programs(0) * span)
    step, cum = head_terms(dt_ref, as_column(rate_ref[...]), t * span, limit)
    last = cum[:, span - 1 :]
    b, c = b_ref[...], c_ref[...]
    x = x_ref[...].astype(F32)
    high, low = split2(x * per_channel(step * jnp.exp(-cum), table))
    lower = iota((span, span), 0) >= iota((span, span), 1)
    score_high, score_low = split2(jnp.where(lower, dot(c, b, 1, 1), 0.0))
    acc = dot(score_high, high, 1, 0) + dot(score_high, low, 1, 0) + dot(score_low, high, 1, 0)
    now = state[...]
    now_high, now_low = split2(now)
    acc = acc + dot(c, now_high, 1, 0) + dot(c, now_low, 1, 0)
    decay = per_channel(jnp.exp(cum), table)
    before = total[...]
    total[...] = before + last
    lane = iota((heads, TILE), 1)
    rows = per_channel(jnp.where(lane < 8, jnp.exp(last), jnp.exp(before)), table)
    live = t * span + iota((span, width), 0) < limit
    gate = jnp.where(live, silu(gate_ref[...].astype(F32)), 0.0)
    part_ref[...] = (acc * decay + skip[0:1] * x) * gate
    coef_ref[...] = decay * rows[8:9] * gate
    state[...] = (now + (dot(b, high, 0, 0) + dot(b, low, 0, 0))) * rows[0:1]


def decode_kernel(turn, *refs):
    part_hbm, coef_hbm = refs[9:11]
    work, (part, coef, sem), store_sem = refs[11:-4], refs[-4:-1], refs[-1]

    @pl.when(lax.axis_index("pool") == turn)
    def _():
        decode_work(*refs[:9], *work, part, coef, sem)
        pairs = ((part, part_hbm), (coef, coef_hbm))
        stores = [pltpu.make_async_copy(*p, store_sem.at[n]) for n, p in enumerate(pairs)]
        for store in stores:
            store.start()
        for store in stores:
            store.wait()


def decode_work(
    slots_hbm, rate_hbm, skip_hbm, dt_hbm, x_hbm, gate_hbm, b_hbm, c_hbm, states_hbm,
    slots_ref, rate_ref, skip_ref, dt_ref, x_ref, gate_ref, b_ref, c_ref, states,
    x_all, gate_all, b_all, c_all, keep_log, size_all, part, coef, sem,
):
    steps, seqs, width = x_ref.shape
    heads = dt_ref.shape[2]
    rows = steps * seqs
    pairs = (
        (slots_hbm, slots_ref), (rate_hbm, rate_ref), (skip_hbm, skip_ref), (dt_hbm, dt_ref),
        (x_hbm, x_ref), (gate_hbm, gate_ref), (b_hbm, b_ref), (c_hbm, c_ref),
        *((states_hbm.at[d], states.at[d]) for d in range(states.shape[0])),
    )
    loads = [pltpu.make_async_copy(*pair, sem.at[n]) for n, pair in enumerate(pairs)]
    for load in loads:
        load.start()
    for load in loads[:-seqs]:
        load.wait()
    total = jnp.zeros((seqs, heads), F32)
    for s in range(steps):
        at = pl.ds(s * seqs, seqs)
        size = jax.nn.softplus(dt_ref[s].astype(F32))
        total = total - size * rate_ref[...]
        keep_log[at, :] = total
        size_all[at, :] = size
        x_all[at, :] = x_ref[s].astype(F32)
        gate_all[at, :] = gate_ref[s].astype(F32)
        b_all[at, :] = b_ref[s].astype(F32)
        c_all[at, :] = c_ref[s].astype(F32)
    table = spread(heads, width)
    keep = exact_dot(jnp.exp(keep_log[...]), table)
    flow = exact_dot(size_all[...] * jnp.exp(-keep_log[...]), table) * x_all[...]
    c = c_all[...].astype(BF16)
    scores = dot(c, b_all[...].astype(BF16), 1, 1)
    row, col = iota((rows, rows), 0), iota((rows, rows), 1)
    same = (row % seqs == col % seqs) & (col <= row)
    inner = exact_dot(jnp.where(same, scores, 0.0), flow)
    skip = exact_dot(jnp.broadcast_to(skip_ref[...], (8, heads)), table)[0:1]
    gate = silu(gate_all[...])
    seq = iota((rows, 1), 0) % seqs
    own = jnp.zeros((rows, width), F32)
    keeps = jnp.zeros((rows, 1), jnp.int32)
    for d in range(seqs):
        loads[d - seqs].wait()
        high, low = split2(states[d])
        mine = (seq == d) & (slots_ref[:, d : d + 1] < 0)
        own = jnp.where(mine, dot(c, high, 1, 1) + dot(c, low, 1, 1), own)
        keeps = jnp.where(mine, 1, keeps)
    part[...] = (keep * (inner + own) + skip * x_all[...]) * gate
    coef[...] = jnp.where(keeps > 0, 0.0, keep * gate)


def mix_kernel(turn, *refs):
    decode, refs = refs[:9], refs[9:]
    coef_hbm, dec_part_hbm, dec_coef_hbm, slots_ref, in_ref, c_ref, part_ref = refs[:7]
    mixed_ref, dec_mixed_ref, power_ref, coef, sem, *work = refs[7:]
    dec_part, dec_coef = work[-3:-1]
    length, width = part_ref.shape
    loads = []
    for t in range(length // SPAN):
        at = pl.ds(t * SPAN, SPAN)
        loads.append(pltpu.make_async_copy(coef_hbm.at[at, :], coef.at[at, :], sem.at[t]))
        loads[-1].start()
    pairs = ((dec_part_hbm, dec_part), (dec_coef_hbm, dec_coef))
    done = [pltpu.make_async_copy(*p, sem.at[len(loads) + n]) for n, p in enumerate(pairs)]

    @pl.when(lax.axis_index("pool") != turn)
    def _():
        for load in done:
            load.start()

    wide = width // TILE
    halves = in_ref.shape[0] // wide
    pieces = [
        jnp.concatenate([in_ref[h * wide + col, :TILE, :] for h in range(halves)], axis=0)
        for col in range(wide)
    ]
    twice = jnp.concatenate(split2(jnp.concatenate(pieces, axis=1)), axis=0)
    power_ref[...] = jnp.zeros_like(power_ref)
    spans = length // SPAN

    def carried(t):
        c = c_ref[t * SPAN : (t + 1) * SPAN, :]
        return dot(jnp.concatenate([c, c], axis=1), twice, 1, 0)

    each = spans // 2
    ready = [carried(t) for t in range(each)]
    for k in range(2):
        now = ready
        for load in loads[k * each : (k + 1) * each]:
            load.wait()
        if k + 1 < 2:
            ready = [carried(t) for t in range((k + 1) * each, (k + 2) * each)]
        for t in range(k * each, (k + 1) * each):
            at = slice(t * SPAN, (t + 1) * SPAN)
            mixed = part_ref[at, :] + coef[at, :] * now[t - k * each]
            mixed_ref[at, :] = mixed
            power_ref[t : t + 1, :] = as_row(jnp.sum(mixed * mixed, axis=1, keepdims=True), SPAN)

    @pl.when(lax.axis_index("pool") != turn)
    def _():
        for load in done:
            load.wait()

    @pl.when(lax.axis_index("pool") == turn)
    def _():
        decode_work(*decode, *work)

    final = jnp.concatenate(
        [in_ref[col, TILE:, :] + in_ref[wide + col, TILE:, :] for col in range(wide)], axis=1
    )
    steps = final.shape[0] // (slots_ref.shape[1] - 1)
    picks = chosen(slots_ref[...], steps)
    final = dot(jnp.concatenate([picks] * 3, axis=0), split3(final), 0, 0)
    dec_mixed = dec_part[...] + dec_coef[...] * final
    dec_mixed_ref[...] = dec_mixed
    power = jnp.sum(dec_mixed * dec_mixed, axis=1, keepdims=True)
    power_ref[4:5, :] = as_row(power, SPAN)


def norm_kernel(
    power_ref, other_ref, gain_ref, mixed_ref, dec_mixed_ref, out_hbm, dec_ref, out, dec, sem
):
    length, width = mixed_ref.shape
    scales = lax.rsqrt((power_ref[...] + other_ref[...]) / (2 * width) + EPS)
    stores = []
    for t in range(length // SPAN):
        at = pl.ds(t * SPAN, SPAN)
        out[at, :] = (mixed_ref[at, :] * as_column(scales[t : t + 1]) * gain_ref[...]).astype(BF16)
        stores.append(pltpu.make_async_copy(out.at[at, :], out_hbm.at[at, :], sem.at[t]))
        stores[-1].start()
    steps, seqs, _ = dec_ref.shape
    rows = steps * seqs
    dec[...] = dec_mixed_ref[...] * as_column(scales[4:5, :TILE])[:rows] * gain_ref[...]
    for s in range(steps):
        dec_ref[s] = dec[s * seqs : (s + 1) * seqs, :].astype(BF16)
    for store in stores:
        store.wait()


def params(mib):
    return pltpu.CompilerParams(
        dimension_semantics=("arbitrary",), vmem_limit_bytes=mib * 2**20
    )


def whole(shape):
    return pl.BlockSpec(shape, lambda t: (0,) * len(shape))


def by_rows(shape):
    return pl.BlockSpec(shape, lambda t: (t,) + (0,) * (len(shape) - 1))


def in_hbm(v):
    return pltpu.with_memory_space_constraint(v, pltpu.HBM)


def in_vmem(v):
    return pltpu.with_memory_space_constraint(v, pltpu.VMEM)


HBM = pl.BlockSpec(memory_space=pltpu.HBM)
VMEM = pl.BlockSpec(memory_space=pltpu.VMEM)
SMEM = pl.BlockSpec(memory_space=pltpu.SMEM)


def cost(flops, mib):
    return pl.CostEstimate(flops=flops, bytes_accessed=mib * 2**20, transcendentals=0)


def device_state(lengths, rate, slots, dt, x, b, dec_c, after, count):
    heads, length = dt.shape
    state, width = b.shape[1], x.shape[1]
    steps, seqs, _ = dec_c.shape
    shape = (count, TILE + 8 + steps * (seqs - 1), TILE)
    return pl.pallas_call(
        state_kernel,
        name="device_state",
        out_shape=pltpu.HBM(shape, F32),
        in_specs=[SMEM] + [HBM] * 7,
        out_specs=HBM,
        scratch_shapes=[
            pltpu.VMEM(rate.shape, F32),
            pltpu.VMEM(slots.shape, jnp.int32),
            pltpu.VMEM(dec_c.shape, BF16),
            pltpu.VMEM((steps * seqs, state), F32),
            pltpu.VMEM((heads, length), BF16),
            pltpu.VMEM((length, width), BF16),
            pltpu.VMEM((length, state), BF16),
            pltpu.VMEM(shape, F32),
            pltpu.SemaphoreType.DMA((9,)),
            pltpu.SemaphoreType.DMA((count,)),
        ],
        compiler_params=pltpu.CompilerParams(vmem_limit_bytes=48 * 2**20),
        cost_estimate=cost(8 * length * state * width, 6),
    )(lengths, *map(in_hbm, (rate, slots, dt, x, b, dec_c, after)))


def device_outputs(lengths, rate, skip, dt, x, gate, b, c):
    heads, length = dt.shape
    state, width = b.shape[1], x.shape[1]
    wide_spec, state_spec = by_rows((SPAN, width)), by_rows((SPAN, state))
    head_spec = whole((1, heads))
    return pl.pallas_call(
        local_kernel,
        name="device_outputs",
        out_shape=[pltpu.HBM((length, width), F32)] * 2,
        grid=(length // SPAN,),
        in_specs=[
            SMEM, head_spec, head_spec, pl.BlockSpec((heads, SPAN), lambda t: (0, t)),
            wide_spec, wide_spec, state_spec, state_spec,
        ],
        out_specs=[wide_spec, wide_spec],
        scratch_shapes=[
            pltpu.VMEM((state, width), F32),
            pltpu.VMEM((heads, TILE), F32),
            pltpu.VMEM((8, width), F32),
        ],
        compiler_params=params(32),
        cost_estimate=cost(20 * length * state * width, 14),
    )(lengths, *map(in_hbm, (rate, skip, dt, x, gate, b, c)))


def decode_scratch(arrays):
    steps, seqs, width = arrays[4].shape
    rows, state, heads = steps * seqs, arrays[6].shape[2], arrays[3].shape[2]
    wide, narrow, small = (pltpu.VMEM((rows, n), F32) for n in (width, state, heads))
    return [
        *(pltpu.VMEM(a.shape, a.dtype) for a in arrays),
        wide, wide, narrow, narrow, small, small, wide, wide,
        pltpu.SemaphoreType.DMA((len(arrays) + arrays[8].shape[0],)),
    ]


def decode_own(turn, arrays):
    steps, seqs, width = arrays[4].shape
    state, rows = arrays[6].shape[2], steps * seqs
    return pl.pallas_call(
        functools.partial(decode_kernel, turn),
        name="decode_own",
        out_shape=[pltpu.HBM((rows, width), F32)] * 2,
        in_specs=[HBM] * len(arrays),
        out_specs=[HBM] * 2,
        scratch_shapes=[*decode_scratch(arrays), pltpu.SemaphoreType.DMA((2,))],
        compiler_params=pltpu.CompilerParams(vmem_limit_bytes=32 * 2**20),
        cost_estimate=cost(4 * seqs * 256 * state * width, 5),
    )(*map(in_hbm, arrays))


def prefix(owned):
    count, rows, _ = owned.shape
    return pl.pallas_call(
        prefix_kernel,
        name="prefix",
        out_shape=jax.ShapeDtypeStruct((count, rows - 8, TILE), F32),
        compiler_params=pltpu.CompilerParams(vmem_limit_bytes=16 * 2**20),
        cost_estimate=cost(2 * count * 32 * TILE * TILE, 3),
    )(owned)


def mix(turn, decode, coef, dec_part, dec_coef, slots, entry, c, part):
    length, width = part.shape
    return pl.pallas_call(
        functools.partial(mix_kernel, turn),
        name="mix",
        out_shape=[
            pltpu.VMEM((length, width), F32),
            pltpu.VMEM(dec_part.shape, F32),
            pltpu.VMEM((8, SPAN), F32),
        ],
        in_specs=[HBM] * 12 + [VMEM] * 4,
        out_specs=[VMEM] * 3,
        scratch_shapes=[
            pltpu.VMEM((length, width), F32),
            pltpu.SemaphoreType.DMA((length // SPAN + 2,)),
            *decode_scratch(decode),
        ],
        compiler_params=pltpu.CompilerParams(vmem_limit_bytes=40 * 2**20),
        cost_estimate=cost(4 * length * c.shape[1] * width, 14),
    )(*map(in_hbm, (*decode, coef, dec_part, dec_coef)), slots, entry, c, part)


def norm(power, other, gain, mixed, dec_mixed, dec_shape):
    length, width = mixed.shape
    return pl.pallas_call(
        norm_kernel,
        name="norm",
        out_shape=[pltpu.HBM((length, width), BF16), jax.ShapeDtypeStruct(dec_shape, BF16)],
        in_specs=[VMEM] * 5,
        out_specs=[HBM, VMEM],
        scratch_shapes=[
            pltpu.VMEM((length, width), BF16),
            pltpu.VMEM(dec_mixed.shape, F32),
            pltpu.SemaphoreType.DMA((length // SPAN,)),
        ],
        compiler_params=pltpu.CompilerParams(vmem_limit_bytes=16 * 2**20),
        cost_estimate=cost(4 * length * width, 6),
    )(power, other, gain, mixed, dec_mixed)


def shards(
    x_in, gate_in, dt_raw, b_in, c_in, lengths, decay_rate, skip_gain, norm_gain,
    dec_states, dec_x, dec_gate, dec_dt, dec_b, dec_c, slots,
):
    _, length, _, width = x_in.shape
    heads, state = dt_raw.shape[3], b_in.shape[3]
    steps, seqs = dec_x.shape[:2]
    count = lax.axis_size(SEQ)
    x, gate = x_in.reshape(length, width), gate_in.reshape(length, width)
    dt = dt_raw.reshape(length, heads).T
    b, c = b_in.reshape(length, state), c_in.reshape(length, state)
    dec_x, dec_gate = dec_x.reshape(steps, seqs, width), dec_gate.reshape(steps, seqs, width)
    dec_b, dec_c = dec_b.reshape(steps, seqs, state), dec_c.reshape(steps, seqs, state)
    dec_dt = dec_dt.reshape(steps, seqs, heads)

    slots_row = slots.reshape(1, seqs)
    decode = (
        slots_row, decay_rate, skip_gain, dec_dt, dec_x, dec_gate, dec_b, dec_c,
        dec_states.reshape(seqs, width, state),
    )
    dec_part, dec_coef = decode_own(0, decode)
    sent = device_state(lengths, decay_rate, slots_row, dt, x, b, dec_c, dec_part, count)
    owned = lax.all_to_all(sent, SEQ, 0, 0)
    part, coef = device_outputs(lengths, decay_rate, skip_gain, dt, x, gate, b, c)
    owned, part, coef = lax.optimization_barrier((owned, part, coef))
    entry = lax.all_to_all(prefix(owned), SEQ, 0, 0)
    mixed, dec_mixed, power = mix(
        1, decode, coef, dec_part, dec_coef, slots_row, entry, c, part
    )
    other = lax.ppermute(power, "pool", [(0, 1), (1, 0)])
    prefill_out, decode_out = norm(
        power, other, norm_gain, mixed, dec_mixed, (steps, seqs, width)
    )
    return prefill_out.reshape(x_in.shape), decode_out.reshape(steps, seqs, 1, width)


def solution(mesh):
    split = Mesh(
        mesh.devices.reshape(mesh.shape["pool"], 4, 4, mesh.shape["head"]),
        ("pool", "seq_0", "seq_1", "head"),
    )
    wide = P(None, SEQ, "head", "pool")
    shared = P(None, SEQ, "head", None)
    per_head = P("head", "pool")
    return jax.shard_map(
        shards,
        mesh=split,
        in_specs=(
            wide, wide, wide, shared, shared, P(), per_head, per_head, per_head,
            P(SEQ, "head", "pool", None, None), wide, wide, wide, shared, shared, P(SEQ),
        ),
        out_specs=(wide, wide),
        check_vma=False,
    )
```
